512 devices in a mesh: mem: 128 (over x, z, core), rep: 4 (over y).
Axes of the slice: x: 4, y: 4, z: 16, core: 2. Of those that a mesh axis runs over, the one named last changes fastest.
Arguments:
- states: bfloat16 [2048, 384], P('rep'), may hold values from -6 to 6
- batch_index: int32 [2, 2048], P(None, 'rep'), may hold values from 0 to 511
- obs_pick: int32 [2, 128], replicated, may hold values from 0 to 383
- norm_gain: float32 [384], replicated, may hold values from 0.5 to 1.5
- w_in: bfloat16 [384, 1024], replicated, may hold values from -0.3125 to 0.3125
- b_in: float32 [1024], replicated, may hold values from -0.5 to 0.5
- member_params: bfloat16 [128, 393216], P('mem', 'rep'), may hold values from -6 to 6
- observed: bfloat16 [2, 2048, 128], P(None, 'rep'), may hold values from -6 to 6
- perturbation: bfloat16 [128, 2, 2048, 128], P('mem', None, 'rep'), may hold values from -6 to 6
- inv_sigma: float32 [2, 2048, 128], P(None, 'rep'), may hold values from 0.5 to 4
Outputs:
- updated_params: bfloat16 [128, 393216], P('mem', 'rep')
The draws below stay inside these ranges and needn't reach their ends.
Inputs may be any that keep to these rules, and one draw needn't show every extreme that they name: `batch_index`: row number of a start state inside the block of 512 given states that belongs to its block of 512 batch rows. `obs_pick`: observed feature numbers; a number may repeat.
All inputs are finite; a program needn't handle non-finite values.
Results may differ from the reference program's by a relative error of at most 0.0056.
Values may be sent and summed in bfloat16 or wider, within the bound.
No kernel may reach another device: no remote copies, remote signals or barrier semaphores. Data moves between devices by JAX's collectives and lax.ppermute only.
A program may use at most 64 MiB of HBM per device.

```python
import math
import jax
import jax.numpy as jnp
from jax import lax

S = 384
H = 1024
OBS_FEAT = 128
STEPS = 2
PASSES = 2
ROWS_DEV = 512
STATES_DEV = 512
MEMBERS = 128
BATCH = 2048
STATE_ROWS = 2048
PARAMS = 393216


def touch_ends(array, key, low, top_value):
    place = [jax.random.randint(jax.random.fold_in(key, axis), (), 0, length) for axis, length in enumerate(array.shape)]
    widest = array.shape.index(max(array.shape))
    neighbour = place[:widest] + [(place[widest] + 1) % array.shape[widest]] + place[widest + 1:]
    return array.at[tuple(place)].set(low).at[tuple(neighbour)].set(top_value)


def shard_levels(stream_key, extent, cuts, least, largest):
    level = 1.0
    for position, shards_of in cuts:
        draws = jax.random.uniform(jax.random.fold_in(jax.random.fold_in(stream_key, 6), position), (shards_of,), jnp.float32, least / len(cuts), largest / len(cuts))
        level = level * jnp.repeat(jnp.exp(draws), extent[position] // shards_of).reshape((-1,) + (1,) * (len(extent) - 1 - position))
    return level


def bell_draw(stream_key, shape, scale, bound, pieces=(), kind=jnp.bfloat16):
    result = scale * jax.random.normal(stream_key, shape, jnp.float32)
    if pieces:
        result = result * shard_levels(stream_key, shape, pieces, -0.22, 0.18)
    return jnp.clip(result, -bound, bound).astype(kind)


def setup_inputs(seed: int = 0) -> dict:
    seeds = jax.random.split(jax.random.key(seed), 11)
    states = bell_draw(seeds[0], (STATE_ROWS, S), 1.0, 6.0, ((0, 4),))
    batch_index = touch_ends(jax.random.randint(seeds[1], (STEPS, BATCH), 0, STATES_DEV), jax.random.fold_in(seeds[1], 1), 0, STATES_DEV - 1).astype(jnp.int32)
    obs_pick = touch_ends(jax.random.randint(seeds[2], (STEPS, OBS_FEAT), 0, S), jax.random.fold_in(seeds[2], 1), 0, S - 1).astype(jnp.int32)
    norm_gain = jnp.clip(1.0 + 0.1 * jax.random.normal(seeds[3], (S,), jnp.float32), 0.5, 1.5)
    w_in = bell_draw(seeds[4], (S, H), S ** -0.5, 0.3125)
    b_in = jnp.clip(jax.random.uniform(seeds[5], (H,), jnp.float32, -0.5, 0.5), -0.5, 0.5)
    member_params = bell_draw(seeds[6], (MEMBERS, PARAMS), 1.0, 6.0, ((0, 128), (1, 4)))
    observed = bell_draw(seeds[7], (STEPS, BATCH, OBS_FEAT), 1.0, 6.0, ((1, 4),))
    perturbation = bell_draw(seeds[8], (MEMBERS, STEPS, BATCH, OBS_FEAT), 1.0, 6.0, ((0, 128), (2, 4)))
    inv_sigma = jnp.clip(jnp.exp(math.log(4.0) - 2.0794415 * jax.random.uniform(seeds[9], (STEPS, BATCH, OBS_FEAT), jnp.float32) ** shard_levels(seeds[9], (STEPS, BATCH, OBS_FEAT), ((1, 4),), -0.2, 0.2)), 0.5, 4.0)
    return {"states": states, "batch_index": batch_index, "obs_pick": obs_pick, "norm_gain": norm_gain, "w_in": w_in, "b_in": b_in, "member_params": member_params, "observed": observed, "perturbation": perturbation, "inv_sigma": inv_sigma}


EPS = 1e-06
DT = 0.5

def hidden_layer(state, norm_gain, w_in, b_in):
    normed = (state * lax.rsqrt(lax.optimization_barrier(jnp.mean(state * state, axis=-1, keepdims=True)) + EPS) * norm_gain).astype(jnp.bfloat16)
    return jax.nn.gelu(jnp.dot(normed.astype(jnp.float32), w_in.astype(jnp.float32), preferred_element_type=jnp.float32) + b_in).astype(jnp.bfloat16)

def reference(states, batch_index, obs_pick, norm_gain, w_in, b_in, member_params, observed, perturbation, inv_sigma):
    block_base = jnp.arange(BATCH, dtype=jnp.int32) // ROWS_DEV * STATES_DEV
    row_numbers = (block_base[None, :] + batch_index).astype(jnp.int32)
    start_state = jnp.take(states, row_numbers, axis=0).astype(jnp.float32)
    shared = hidden_layer(start_state, norm_gain, w_in, b_in)
    step_scale = DT * H ** (-0.5)
    picks = jnp.broadcast_to(obs_pick[:, None, :], (STEPS, BATCH, OBS_FEAT)).astype(jnp.int32)

    def one_member(inputs):
        params, noise_row = inputs
        weights = params.reshape(H, S)
        current = start_state + step_scale * jnp.dot(shared.astype(jnp.float32), weights.astype(jnp.float32), preferred_element_type=jnp.float32)
        for pass_index in range(PASSES - 1):
            layer = hidden_layer(current, norm_gain, w_in, b_in)
            current = current + step_scale * jnp.dot(layer.astype(jnp.float32), weights.astype(jnp.float32), preferred_element_type=jnp.float32)
        predicted = jnp.take_along_axis(current, picks, axis=2)
        weighted = (predicted * inv_sigma).astype(jnp.bfloat16)
        misfit_w = (observed.astype(jnp.float32) * inv_sigma + noise_row.astype(jnp.float32) - predicted * inv_sigma).astype(jnp.bfloat16)
        return (weighted, misfit_w)
    weighted, misfit_w = lax.map(one_member, (member_params, perturbation))
    flat = weighted.reshape(MEMBERS, -1).astype(jnp.float32)
    anomaly = (flat - lax.optimization_barrier(jnp.mean(flat, axis=0))).astype(jnp.bfloat16)
    misfit_flat = misfit_w.reshape(MEMBERS, -1)
    gram_matrix = jnp.dot(anomaly.astype(jnp.float32), anomaly.T.astype(jnp.float32), preferred_element_type=jnp.float32)
    innovation = jnp.dot(anomaly.astype(jnp.float32), misfit_flat.T.astype(jnp.float32), preferred_element_type=jnp.float32)
    misfit = jnp.mean(jnp.square(misfit_flat.astype(jnp.float32)))
    system = gram_matrix + (1.0 + misfit) * (MEMBERS - 1) * jnp.eye(MEMBERS, dtype=jnp.float32)
    lower_factor = jnp.linalg.cholesky(system)
    halfway = lax.linalg.triangular_solve(lower_factor, innovation, left_side=True, lower=True)
    coefficients = lax.linalg.triangular_solve(lower_factor, halfway, left_side=True, lower=True, transpose_a=True)
    params_f = member_params.astype(jnp.float32)
    spread = params_f - lax.optimization_barrier(jnp.mean(params_f, axis=0))
    change = jnp.einsum('kj,kp->jp', coefficients, spread, precision=lax.Precision.HIGHEST)
    return (params_f + change).astype(jnp.bfloat16)
```

```python
import jax
import jax.numpy as jnp
from jax import lax
from jax.sharding import Mesh
from jax.sharding import PartitionSpec as P

EPS = 1e-06
DT = 0.5
MEM = ("x", "z", "c")
NEAR = ("x", "c", "r")
HIGHEST = lax.Precision.HIGHEST


def hidden_layer(state, norm_gain, w_in, b_in):
    normed = (
        state * lax.rsqrt(jnp.mean(state * state, axis=-1, keepdims=True) + EPS) * norm_gain
    ).astype(jnp.bfloat16)
    return jax.nn.gelu(jnp.dot(normed, w_in, preferred_element_type=jnp.float32) + b_in).astype(
        jnp.bfloat16
    )


def solve_columns(system, right_side):
    lower_factor = jnp.linalg.cholesky(system)
    halfway = lax.linalg.triangular_solve(lower_factor, right_side, left_side=True, lower=True)
    return lax.linalg.triangular_solve(
        lower_factor, halfway, left_side=True, lower=True, transpose_a=True
    )


def exchange(value, axes):
    return lax.all_to_all(value, axes, split_axis=0, concat_axis=0, tiled=True)


def spread_to(value, axes):
    count = lax.axis_size(axes)
    return exchange(jnp.broadcast_to(value[None], (count,) + value.shape), axes)


def total_of(partial):
    near = lax.axis_size(NEAR)
    piece = jnp.sum(exchange(partial.reshape(near, -1, partial.shape[1]), NEAR), axis=0)
    piece = jnp.sum(spread_to(piece, "z"), axis=0)
    return spread_to(piece, NEAR).reshape(partial.shape)


def on_device(
    states,
    batch_index,
    obs_pick,
    norm_gain,
    w_in,
    b_in,
    member_params,
    observed,
    perturbation,
    inv_sigma,
):
    members = lax.axis_size(MEM)
    width = w_in.shape[1]
    features = w_in.shape[0]
    step_count, rows = batch_index.shape
    picked = obs_pick.shape[1]
    own = member_params.reshape(-1, features)
    weights = lax.all_gather(own, "r", axis=0, tiled=True)
    noise = exchange(perturbation.reshape(members, -1, picked), MEM)
    param_block = exchange(own.reshape(members, -1, features), MEM)
    step_scale = DT * width ** (-0.5)
    current = states.astype(jnp.float32)
    for _ in range(2):
        layer = hidden_layer(current, norm_gain, w_in, b_in)
        current = current + step_scale * jnp.dot(layer, weights, preferred_element_type=jnp.float32)
    feature_ids = lax.broadcasted_iota(jnp.int32, (step_count, features, picked), 1)
    selector = (feature_ids == obs_pick[:, None, :]).astype(jnp.float32)
    state_ids = lax.broadcasted_iota(jnp.int32, (step_count, rows, states.shape[0]), 2)
    row_selector = (state_ids == batch_index[:, :, None]).astype(jnp.float32)
    narrowed = jnp.einsum("bs,ksf->kbf", current, selector, precision=HIGHEST)
    predicted = jnp.einsum("kib,kbf->kif", row_selector, narrowed, precision=HIGHEST)
    scaled = predicted * inv_sigma
    aim = observed.astype(jnp.float32) * inv_sigma
    weighted = scaled.astype(jnp.bfloat16)
    misfit_w = (aim + perturbation[0].astype(jnp.float32) - scaled).astype(jnp.bfloat16)
    misfit_local = jnp.sum(jnp.square(misfit_w.astype(jnp.float32)))
    entries = members * step_count * rows * lax.axis_size("r") * picked
    gathered = exchange(weighted.reshape(members, -1, picked), MEM).astype(jnp.float32)
    depth = gathered.shape[1]
    place = lax.axis_index(MEM) * depth
    aim_here = lax.dynamic_slice_in_dim(aim.reshape(-1, picked), place, depth, 0)
    anomaly = (gathered - jnp.mean(gathered, axis=0)).astype(jnp.bfloat16)
    misfit_here = (aim_here + noise.astype(jnp.float32) - gathered).astype(jnp.bfloat16)
    both = jnp.concatenate([anomaly, misfit_here], axis=0)
    partial = lax.dot_general(
        both, anomaly, (((1, 2), (1, 2)), ((), ())), preferred_element_type=jnp.float32
    )
    unit = lax.broadcasted_iota(jnp.int32, partial.shape, 0) == lax.broadcasted_iota(
        jnp.int32, partial.shape, 1
    )
    partial = partial + jnp.where(unit, misfit_local * ((members - 1) / entries), 0.0)
    total = total_of(partial)
    system = total[:members] + (members - 1.0) * jnp.eye(members, dtype=jnp.float32)
    coefficients = solve_columns(system, total[members:].T)
    centred = coefficients - jnp.mean(coefficients, axis=0)
    params_f = param_block.astype(jnp.float32)
    change = jnp.einsum("kj,kap->jap", centred, params_f, precision=HIGHEST)
    renewed = (params_f + change).astype(jnp.bfloat16)
    return exchange(renewed, MEM).reshape(member_params.shape)


def solution(mesh):
    fine = Mesh(mesh.devices.reshape(4, 16, 2, 4), ("x", "z", "c", "r"))
    placed = (
        P("r", None),
        P(None, "r"),
        P(),
        P(),
        P(),
        P(),
        P(MEM, "r"),
        P(None, "r", None),
        P(MEM, None, "r", None),
        P(None, "r", None),
    )
    return jax.shard_map(
        on_device, mesh=fine, in_specs=placed, out_specs=P(MEM, "r"), check_vma=False
    )
```

```python
import jax
import jax.numpy as jnp
from jax import lax
from jax.experimental import pallas as pl
from jax.experimental.pallas import tpu as pltpu
from jax.sharding import Mesh
from jax.sharding import PartitionSpec as P

EPS = 1e-06
DT = 0.5
MEM = ("x", "z", "c")
NEAR = ("x", "c", "r")
BLOCK = 8
HIGHEST = lax.Precision.HIGHEST


def hidden_layer(state, norm_gain, w_in, b_in):
    normed = (
        state * lax.rsqrt(jnp.mean(state * state, axis=-1, keepdims=True) + EPS) * norm_gain
    ).astype(jnp.bfloat16)
    return jax.nn.gelu(jnp.dot(normed, w_in, preferred_element_type=jnp.float32) + b_in).astype(
        jnp.bfloat16
    )


def eliminate(left, right):
    wide = lambda v: jnp.broadcast_to(v, left[0].shape)
    cols = [[wide(tile[:, q : q + 1]) for q in range(BLOCK)] for tile in left]
    pivots = [[wide(cols[0][q][p : p + 1]) for q in range(BLOCK)] for p in range(BLOCK)]
    top = [wide(left[0][p : p + 1]) for p in range(BLOCK)]
    side = [wide(right[0][p : p + 1]) for p in range(BLOCK)]
    for p in range(BLOCK):
        inverse = 1.0 / pivots[p][p]
        for c in range(p + 1, BLOCK):
            pivots[p][c] = pivots[p][c] * inverse
        top[p] = top[p] * inverse
        side[p] = side[p] * inverse
        for q in range(BLOCK):
            if q != p:
                factor = pivots[q][p]
                for c in range(p + 1, BLOCK):
                    pivots[q][c] = pivots[q][c] - factor * pivots[p][c]
                top[q] = top[q] - factor * top[p]
                side[q] = side[q] - factor * side[p]
    row = lax.broadcasted_iota(jnp.int32, left[0].shape, 0)
    last_left, last_right = top[0], side[0]
    for p in range(1, BLOCK):
        last_left = jnp.where(row == p, top[p], last_left)
        last_right = jnp.where(row == p, side[p], last_right)
    next_left, next_right = [], []
    for t in range(1, len(left)):
        a, b = left[t], right[t]
        for q in range(BLOCK):
            a = a - cols[t][q] * top[q]
            b = b - cols[t][q] * side[q]
        next_left.append(a)
        next_right.append(b)
    next_left.append(last_left)
    next_right.append(last_right)
    turn = left[0].shape[1] - BLOCK
    return [pltpu.roll(a, turn, 1) for a in next_left], next_right


def solve_kernel(total_ref, out_ref):
    n = out_ref.shape[0]
    row = lax.broadcasted_iota(jnp.int32, (n, n), 0)
    column = lax.broadcasted_iota(jnp.int32, (n, n), 1)
    system = total_ref[:n] + jnp.where(row == column, n - 1.0, 0.0)
    right_side = total_ref[n:].T
    left = [system[t : t + BLOCK] for t in range(0, n, BLOCK)]
    right = [right_side[t : t + BLOCK] for t in range(0, n, BLOCK)]
    _, solved = lax.fori_loop(0, n // BLOCK, lambda _, lr: eliminate(*lr), (left, right))
    solved = jnp.concatenate(solved, axis=0)
    out_ref[...] = solved - jnp.mean(solved, axis=0, keepdims=True)


def centred_coefficients(total):
    n = total.shape[1]
    return pl.pallas_call(
        solve_kernel,
        out_shape=jax.ShapeDtypeStruct((n, n), jnp.float32),
        cost_estimate=pl.CostEstimate(flops=40000000, bytes_accessed=200000, transcendentals=0),
        compiler_params=pltpu.CompilerParams(vmem_limit_bytes=4 * 1024 * 1024),
    )(total)


def exchange(value, axes):
    return lax.all_to_all(value, axes, split_axis=0, concat_axis=0, tiled=True)


def spread_to(value, axes):
    count = lax.axis_size(axes)
    return exchange(jnp.broadcast_to(value[None], (count,) + value.shape), axes)


def total_of(partial):
    near = lax.axis_size(NEAR)
    piece = jnp.sum(exchange(partial.reshape(near, -1, partial.shape[1]), NEAR), axis=0)
    piece = jnp.sum(spread_to(piece, "z"), axis=0)
    return spread_to(piece, NEAR).reshape(partial.shape)


def on_device(
    states,
    batch_index,
    obs_pick,
    norm_gain,
    w_in,
    b_in,
    member_params,
    observed,
    perturbation,
    inv_sigma,
):
    members = lax.axis_size(MEM)
    width = w_in.shape[1]
    features = w_in.shape[0]
    step_count, rows = batch_index.shape
    picked = obs_pick.shape[1]
    own = member_params.reshape(-1, features)
    weights = lax.all_gather(own, "r", axis=0, tiled=True)
    noise = exchange(perturbation.reshape(members, -1, picked), MEM)
    param_block = exchange(own.reshape(members, -1, features), MEM)
    step_scale = DT * width ** (-0.5)
    current = states.astype(jnp.float32)
    for turn in range(2):
        if turn:
            current, noise = lax.optimization_barrier((current, noise))
        layer = hidden_layer(current, norm_gain, w_in, b_in)
        current = current + step_scale * jnp.dot(layer, weights, preferred_element_type=jnp.float32)
    feature_ids = lax.broadcasted_iota(jnp.int32, (step_count, features, picked), 1)
    selector = (feature_ids == obs_pick[:, None, :]).astype(jnp.float32)
    state_ids = lax.broadcasted_iota(jnp.int32, (step_count, rows, states.shape[0]), 2)
    row_selector = (state_ids == batch_index[:, :, None]).astype(jnp.float32)
    narrowed = jnp.einsum("bs,ksf->kbf", current, selector, precision=HIGHEST)
    predicted = jnp.einsum("kib,kbf->kif", row_selector, narrowed, precision=HIGHEST)
    scaled = predicted * inv_sigma
    aim = observed.astype(jnp.float32) * inv_sigma
    weighted = scaled.astype(jnp.bfloat16)
    misfit_w = (aim + perturbation[0].astype(jnp.float32) - scaled).astype(jnp.bfloat16)
    misfit_local = jnp.sum(jnp.square(misfit_w.astype(jnp.float32)))
    entries = members * step_count * rows * lax.axis_size("r") * picked
    gathered = exchange(weighted.reshape(members, -1, picked), MEM).astype(jnp.float32)
    depth = gathered.shape[1]
    place = lax.axis_index(MEM) * depth
    aim_here = lax.dynamic_slice_in_dim(aim.reshape(-1, picked), place, depth, 0)
    anomaly = (gathered - jnp.mean(gathered, axis=0)).astype(jnp.bfloat16)
    misfit_here = (aim_here + noise.astype(jnp.float32) - gathered).astype(jnp.bfloat16)
    both = jnp.concatenate([anomaly, misfit_here], axis=0)
    partial = lax.dot_general(
        both, anomaly, (((1, 2), (1, 2)), ((), ())), preferred_element_type=jnp.float32
    )
    unit = lax.broadcasted_iota(jnp.int32, partial.shape, 0) == lax.broadcasted_iota(
        jnp.int32, partial.shape, 1
    )
    partial = partial + jnp.where(unit, misfit_local * ((members - 1) / entries), 0.0)
    total = total_of(partial)
    centred = centred_coefficients(total)
    params_f = param_block.astype(jnp.float32)
    change = jnp.einsum("kj,kap->jap", centred, params_f, precision=HIGHEST)
    renewed = (params_f + change).astype(jnp.bfloat16)
    return exchange(renewed, MEM).reshape(member_params.shape)


def solution(mesh):
    fine = Mesh(mesh.devices.reshape(4, 16, 2, 4), ("x", "z", "c", "r"))
    placed = (
        P("r", None),
        P(None, "r"),
        P(),
        P(),
        P(),
        P(),
        P(MEM, "r"),
        P(None, "r", None),
        P(MEM, None, "r", None),
        P(None, "r", None),
    )
    return jax.shard_map(
        on_device, mesh=fine, in_specs=placed, out_specs=P(MEM, "r"), check_vma=False
    )
```

```python
import jax
import jax.numpy as jnp
from jax import lax
from jax.experimental import pallas as pl
from jax.experimental.pallas import tpu as pltpu
from jax.sharding import Mesh
from jax.sharding import PartitionSpec as P

EPS = 1e-06
DT = 0.5
MEM = ("z", "x", "c")
PAIR = ("x", "c")
OWNERS = ("x", "z", "c")
NEAR = ("x", "c", "r")
BLOCK = 8
HIGHEST = lax.Precision.HIGHEST


def hidden_layer(state, norm_gain, w_in, b_in):
    normed = (
        state * lax.rsqrt(jnp.mean(state * state, axis=-1, keepdims=True) + EPS) * norm_gain
    ).astype(jnp.bfloat16)
    return jax.nn.gelu(jnp.dot(normed, w_in, preferred_element_type=jnp.float32) + b_in).astype(
        jnp.bfloat16
    )


def eliminate(left, right):
    wide = lambda v: jnp.broadcast_to(v, left[0].shape)
    cols = [[wide(tile[:, q : q + 1]) for q in range(BLOCK)] for tile in left]
    pivots = [[wide(cols[0][q][p : p + 1]) for q in range(BLOCK)] for p in range(BLOCK)]
    top = [wide(left[0][p : p + 1]) for p in range(BLOCK)]
    side = [wide(right[0][p : p + 1]) for p in range(BLOCK)]
    for p in range(BLOCK):
        inverse = 1.0 / pivots[p][p]
        for c in range(p + 1, BLOCK):
            pivots[p][c] = pivots[p][c] * inverse
        top[p] = top[p] * inverse
        side[p] = side[p] * inverse
        for q in range(BLOCK):
            if q != p:
                factor = pivots[q][p]
                for c in range(p + 1, BLOCK):
                    pivots[q][c] = pivots[q][c] - factor * pivots[p][c]
                top[q] = top[q] - factor * top[p]
                side[q] = side[q] - factor * side[p]
    row = lax.broadcasted_iota(jnp.int32, left[0].shape, 0)
    last_left, last_right = top[0], side[0]
    for p in range(1, BLOCK):
        last_left = jnp.where(row == p, top[p], last_left)
        last_right = jnp.where(row == p, side[p], last_right)
    next_left, next_right = [], []
    for t in range(1, len(left)):
        a, b = left[t], right[t]
        for q in range(BLOCK):
            a = a - cols[t][q] * top[q]
            b = b - cols[t][q] * side[q]
        next_left.append(a)
        next_right.append(b)
    next_left.append(last_left)
    next_right.append(last_right)
    turn = left[0].shape[1] - BLOCK
    return [pltpu.roll(a, turn, 1) for a in next_left], next_right


def solve_kernel(first_ref, total_ref, out_ref):
    n = total_ref.shape[1]
    few = out_ref.shape[0] // 3
    row = lax.broadcasted_iota(jnp.int32, (n, n), 0)
    column = lax.broadcasted_iota(jnp.int32, (n, n), 1)
    system = total_ref[:n] + jnp.where(row == column, n - 1.0, 0.0)
    first = pl.multiple_of(n + first_ref[0] * few, few)
    right_side = jnp.concatenate([total_ref[pl.ds(first, few), :]] * (n // few), axis=0).T
    left = [system[t : t + BLOCK] for t in range(0, n, BLOCK)]
    right = [right_side[t : t + BLOCK] for t in range(0, n, BLOCK)]
    _, solved = lax.fori_loop(0, n // BLOCK, lambda _, lr: eliminate(*lr), (left, right))
    solved = jnp.concatenate(solved, axis=0)
    rest = (solved - jnp.mean(solved, axis=0, keepdims=True)).T[:few]
    for part in range(3):
        head = rest.astype(jnp.bfloat16).astype(jnp.float32)
        out_ref[part * few : (part + 1) * few] = head
        rest = rest - head


def centred_coefficients(total, first, few):
    n = total.shape[1]
    return pl.pallas_call(
        solve_kernel,
        out_shape=jax.ShapeDtypeStruct((3 * few, n), jnp.float32),
        in_specs=[
            pl.BlockSpec(memory_space=pltpu.SMEM),
            pl.BlockSpec(memory_space=pltpu.VMEM),
        ],
        out_specs=pl.BlockSpec(memory_space=pltpu.VMEM),
        cost_estimate=pl.CostEstimate(flops=40000000, bytes_accessed=200000, transcendentals=0),
        compiler_params=pltpu.CompilerParams(vmem_limit_bytes=4 * 1024 * 1024),
    )(first, total)


def exchange(value, axes):
    return lax.all_to_all(value, axes, split_axis=0, concat_axis=0, tiled=True)


def spread_to(value, axes):
    count = lax.axis_size(axes)
    return exchange(jnp.broadcast_to(value[None], (count,) + value.shape), axes)


def total_of(partial):
    near = lax.axis_size(NEAR)
    piece = jnp.sum(exchange(partial.reshape(near, -1, partial.shape[1]), NEAR), axis=0)
    piece = jnp.sum(spread_to(piece, "z"), axis=0)
    return spread_to(piece, NEAR).reshape(partial.shape)


def on_device(
    states,
    batch_index,
    obs_pick,
    norm_gain,
    w_in,
    b_in,
    member_params,
    observed,
    perturbation,
    inv_sigma,
):
    members = lax.axis_size(MEM)
    width = w_in.shape[1]
    features = w_in.shape[0]
    step_count, rows = batch_index.shape
    picked = obs_pick.shape[1]
    own = member_params.reshape(-1, features)
    weights = lax.all_gather(own, "r", axis=0, tiled=True)
    few = lax.axis_size(PAIR)
    piece = exchange(member_params.reshape(few, -1), PAIR)
    perturbation, piece = lax.optimization_barrier((perturbation, piece))
    noise = exchange(perturbation.reshape(members, -1, picked), MEM)
    everyone = lax.all_gather(piece, "z", axis=0, tiled=True)
    step_scale = DT * width ** (-0.5)
    current = states.astype(jnp.float32)
    for turn in range(2):
        if turn:
            current, noise = lax.optimization_barrier((current, noise))
        layer = hidden_layer(current, norm_gain, w_in, b_in)
        current = current + step_scale * jnp.dot(layer, weights, preferred_element_type=jnp.float32)
    feature_ids = lax.broadcasted_iota(jnp.int32, (step_count, features, picked), 1)
    selector = (feature_ids == obs_pick[:, None, :]).astype(jnp.float32)
    state_ids = lax.broadcasted_iota(jnp.int32, (step_count, rows, states.shape[0]), 2)
    row_selector = (state_ids == batch_index[:, :, None]).astype(jnp.float32)
    narrowed = jnp.einsum("bs,ksf->kbf", current, selector, precision=HIGHEST)
    predicted = jnp.einsum("kib,kbf->kif", row_selector, narrowed, precision=HIGHEST)
    scaled = predicted * inv_sigma
    aim = observed.astype(jnp.float32) * inv_sigma
    weighted = scaled.astype(jnp.bfloat16)
    misfit_w = (aim + perturbation[0].astype(jnp.float32) - scaled).astype(jnp.bfloat16)
    misfit_local = jnp.sum(jnp.square(misfit_w.astype(jnp.float32)))
    entries = members * step_count * rows * lax.axis_size("r") * picked
    gathered = exchange(weighted.reshape(members, -1, picked), MEM).astype(jnp.float32)
    depth = gathered.shape[1]
    place = lax.axis_index(MEM) * depth
    aim_here = lax.dynamic_slice_in_dim(aim.reshape(-1, picked), place, depth, 0)
    anomaly = (gathered - jnp.mean(gathered, axis=0)).astype(jnp.bfloat16)
    misfit_here = (aim_here + noise.astype(jnp.float32) - gathered).astype(jnp.bfloat16)
    both = jnp.concatenate([anomaly, misfit_here], axis=0)
    partial = lax.dot_general(
        both, anomaly, (((1, 2), (1, 2)), ((), ())), preferred_element_type=jnp.float32
    )
    unit = lax.broadcasted_iota(jnp.int32, partial.shape, 0) == lax.broadcasted_iota(
        jnp.int32, partial.shape, 1
    )
    partial = partial + jnp.where(unit, misfit_local * ((members - 1) / entries), 0.0)
    total = total_of(partial)
    parts = centred_coefficients(total, lax.axis_index("z").reshape(1), few)
    change = jnp.dot(parts.astype(jnp.bfloat16), everyone, preferred_element_type=jnp.float32)
    change = jnp.sum(change.reshape(3, few, -1), axis=0)
    renewed = (piece.astype(jnp.float32) + change).astype(jnp.bfloat16)
    return exchange(renewed, PAIR).reshape(member_params.shape)


def solution(mesh):
    fine = Mesh(mesh.devices.reshape(4, 16, 2, 4), ("x", "z", "c", "r"))
    placed = (
        P("r", None),
        P(None, "r"),
        P(),
        P(),
        P(),
        P(),
        P(OWNERS, "r"),
        P(None, "r", None),
        P(OWNERS, None, "r", None),
        P(None, "r", None),
    )
    return jax.shard_map(
        on_device, mesh=fine, in_specs=placed, out_specs=P(OWNERS, "r"), check_vma=False
    )
```

```python
import jax
import jax.numpy as jnp
from jax import lax
from jax.experimental import pallas as pl
from jax.experimental.pallas import tpu as pltpu
from jax.sharding import Mesh
from jax.sharding import PartitionSpec as P

EPS = 1e-06
DT = 0.5
MEM = ("z", "x", "c")
PAIR = ("x", "c")
OWNERS = ("x", "z", "c")
NEAR = ("x", "c", "r")
BLOCK = 8
HIGHEST = lax.Precision.HIGHEST


def hidden_layer(state, norm_gain, w_in, b_in):
    normed = (
        state * lax.rsqrt(jnp.mean(state * state, axis=-1, keepdims=True) + EPS) * norm_gain
    ).astype(jnp.bfloat16)
    return jax.nn.gelu(jnp.dot(normed, w_in, preferred_element_type=jnp.float32) + b_in).astype(
        jnp.bfloat16
    )


def eliminate(left, right):
    wide = lambda v: jnp.broadcast_to(v, left[0].shape)
    cols = [[wide(tile[:, q : q + 1]) for q in range(BLOCK)] for tile in left]
    pivots = [[wide(cols[0][q][p : p + 1]) for q in range(BLOCK)] for p in range(BLOCK)]
    top = [wide(left[0][p : p + 1]) for p in range(BLOCK)]
    side = [wide(right[0][p : p + 1]) for p in range(BLOCK)]
    for p in range(BLOCK):
        inverse = 1.0 / pivots[p][p]
        for c in range(p + 1, BLOCK):
            pivots[p][c] = pivots[p][c] * inverse
        top[p] = top[p] * inverse
        side[p] = side[p] * inverse
        for q in range(BLOCK):
            if q != p:
                factor = pivots[q][p]
                for c in range(p + 1, BLOCK):
                    pivots[q][c] = pivots[q][c] - factor * pivots[p][c]
                top[q] = top[q] - factor * top[p]
                side[q] = side[q] - factor * side[p]
    row = lax.broadcasted_iota(jnp.int32, left[0].shape, 0)
    last_left, last_right = top[0], side[0]
    for p in range(1, BLOCK):
        last_left = jnp.where(row == p, top[p], last_left)
        last_right = jnp.where(row == p, side[p], last_right)
    next_left, next_right = [], []
    for t in range(1, len(left)):
        a, b = left[t], right[t]
        for q in range(BLOCK):
            a = a - cols[t][q] * top[q]
            b = b - cols[t][q] * side[q]
        next_left.append(a)
        next_right.append(b)
    next_left.append(last_left)
    next_right.append(last_right)
    turn = left[0].shape[1] - BLOCK
    return [pltpu.roll(a, turn, 1) for a in next_left], next_right


def solve_kernel(first_ref, total_ref, out_ref):
    n = total_ref.shape[1]
    few = out_ref.shape[0] // 3
    row = lax.broadcasted_iota(jnp.int32, (n, n), 0)
    column = lax.broadcasted_iota(jnp.int32, (n, n), 1)
    system = total_ref[:n] + jnp.where(row == column, n - 1.0, 0.0)
    first = pl.multiple_of(n + first_ref[0] * few, few)
    right_side = jnp.concatenate([total_ref[pl.ds(first, few), :]] * (n // few), axis=0).T
    left = [system[t : t + BLOCK] for t in range(0, n, BLOCK)]
    right = [right_side[t : t + BLOCK] for t in range(0, n, BLOCK)]
    _, solved = lax.fori_loop(0, n // BLOCK, lambda _, lr: eliminate(*lr), (left, right))
    solved = jnp.concatenate(solved, axis=0)
    rest = (solved - jnp.mean(solved, axis=0, keepdims=True)).T[:few]
    for part in range(3):
        head = rest.astype(jnp.bfloat16).astype(jnp.float32)
        out_ref[part * few : (part + 1) * few] = head
        rest = rest - head


def centred_coefficients(total, first, few):
    n = total.shape[1]
    return pl.pallas_call(
        solve_kernel,
        out_shape=jax.ShapeDtypeStruct((3 * few, n), jnp.float32),
        in_specs=[
            pl.BlockSpec(memory_space=pltpu.SMEM),
            pl.BlockSpec(memory_space=pltpu.VMEM),
        ],
        out_specs=pl.BlockSpec(memory_space=pltpu.VMEM),
        cost_estimate=pl.CostEstimate(flops=40000000, bytes_accessed=200000, transcendentals=0),
        compiler_params=pltpu.CompilerParams(vmem_limit_bytes=4 * 1024 * 1024),
    )(first, total)


def exchange(value, axes):
    return lax.all_to_all(value, axes, split_axis=0, concat_axis=0, tiled=True)


def spread_to(value, axes):
    count = lax.axis_size(axes)
    return exchange(jnp.broadcast_to(value[None], (count,) + value.shape), axes)


def total_of(partial):
    near = lax.axis_size(NEAR)
    piece = jnp.sum(exchange(partial.reshape(near, -1, partial.shape[1]), NEAR), axis=0)
    piece = jnp.sum(spread_to(piece, "z"), axis=0)
    return spread_to(piece, NEAR).reshape(partial.shape)


def on_device(
    states,
    batch_index,
    obs_pick,
    norm_gain,
    w_in,
    b_in,
    member_params,
    observed,
    perturbation,
    inv_sigma,
):
    members = lax.axis_size(MEM)
    width = w_in.shape[1]
    features = w_in.shape[0]
    step_count, rows = batch_index.shape
    picked = obs_pick.shape[1]
    own = member_params.reshape(-1, features)
    few = lax.axis_size(PAIR)
    piece = exchange(own.reshape(few, -1, features), PAIR)
    weights = lax.all_gather(own, "r", axis=0, tiled=True)
    piece, weights = lax.optimization_barrier((piece, weights))
    piece = piece.reshape(few, -1)
    everyone = lax.all_gather(piece, "z", axis=0, tiled=True)
    step_scale = DT * width ** (-0.5)
    current = states.astype(jnp.float32)
    for _ in range(2):
        layer = hidden_layer(current, norm_gain, w_in, b_in)
        current = current + step_scale * jnp.dot(layer, weights, preferred_element_type=jnp.float32)
    feature_ids = lax.broadcasted_iota(jnp.int32, (step_count, features, picked), 1)
    selector = (feature_ids == obs_pick[:, None, :]).astype(jnp.float32)
    state_ids = lax.broadcasted_iota(jnp.int32, (step_count, rows, states.shape[0]), 2)
    row_selector = (state_ids == batch_index[:, :, None]).astype(jnp.float32)
    narrowed = jnp.einsum("bs,ksf->kbf", current, selector, precision=HIGHEST)
    predicted = jnp.einsum("kib,kbf->kif", row_selector, narrowed, precision=HIGHEST)
    scaled = predicted * inv_sigma
    weighted = scaled.astype(jnp.bfloat16)
    misfit_w = (
        observed.astype(jnp.float32) * inv_sigma + perturbation[0].astype(jnp.float32) - scaled
    ).astype(jnp.bfloat16)
    misfit_local = jnp.sum(jnp.square(misfit_w.astype(jnp.float32)))
    entries = members * step_count * rows * lax.axis_size("r") * picked
    sent = jnp.concatenate(
        [weighted.reshape(members, -1, picked), misfit_w.reshape(members, -1, picked)], axis=1
    )
    gathered, misfit_here = jnp.split(exchange(sent, MEM), 2, axis=1)
    gathered = gathered.astype(jnp.float32)
    anomaly = (gathered - jnp.mean(gathered, axis=0)).astype(jnp.bfloat16)
    both = jnp.concatenate([anomaly, misfit_here], axis=0)
    partial = lax.dot_general(
        both, anomaly, (((1, 2), (1, 2)), ((), ())), preferred_element_type=jnp.float32
    )
    unit = lax.broadcasted_iota(jnp.int32, partial.shape, 0) == lax.broadcasted_iota(
        jnp.int32, partial.shape, 1
    )
    partial = partial + jnp.where(unit, misfit_local * ((members - 1) / entries), 0.0)
    total = total_of(partial)
    parts = centred_coefficients(total, lax.axis_index("z").reshape(1), few)
    change = jnp.dot(parts.astype(jnp.bfloat16), everyone, preferred_element_type=jnp.float32)
    change = jnp.sum(change.reshape(3, few, -1), axis=0)
    renewed = (piece.astype(jnp.float32) + change).astype(jnp.bfloat16)
    return exchange(renewed, PAIR).reshape(member_params.shape)


def solution(mesh):
    fine = Mesh(mesh.devices.reshape(4, 16, 2, 4), ("x", "z", "c", "r"))
    placed = (
        P("r", None),
        P(None, "r"),
        P(),
        P(),
        P(),
        P(),
        P(OWNERS, "r"),
        P(None, "r", None),
        P(OWNERS, None, "r", None),
        P(None, "r", None),
    )
    return jax.shard_map(
        on_device, mesh=fine, in_specs=placed, out_specs=P(OWNERS, "r"), check_vma=False
    )
```

```python
import jax
import jax.numpy as jnp
from jax import lax
from jax.experimental import pallas as pl
from jax.experimental.pallas import tpu as pltpu
from jax.sharding import Mesh
from jax.sharding import PartitionSpec as P

EPS = 1e-06
DT = 0.5
MEM = ("z", "x", "c")
OWNERS = ("x", "z", "c")
NEAR = ("x", "c", "r")
BLOCK = 8
HIGHEST = lax.Precision.HIGHEST


def hidden_layer(state, norm_gain, w_in, b_in):
    normed = (
        state * lax.rsqrt(jnp.mean(state * state, axis=-1, keepdims=True) + EPS) * norm_gain
    ).astype(jnp.bfloat16)
    return jax.nn.gelu(jnp.dot(normed, w_in, preferred_element_type=jnp.float32) + b_in).astype(
        jnp.bfloat16
    )


def eliminate(left, right):
    wide = lambda v: jnp.broadcast_to(v, left[0].shape)
    cols = [[wide(tile[:, q : q + 1]) for q in range(BLOCK)] for tile in left]
    pivots = [[wide(cols[0][q][p : p + 1]) for q in range(BLOCK)] for p in range(BLOCK)]
    top = [wide(left[0][p : p + 1]) for p in range(BLOCK)]
    side = [wide(right[0][p : p + 1]) for p in range(BLOCK)]
    for p in range(BLOCK):
        inverse = 1.0 / pivots[p][p]
        for c in range(p + 1, BLOCK):
            pivots[p][c] = pivots[p][c] * inverse
        top[p] = top[p] * inverse
        side[p] = side[p] * inverse
        for q in range(BLOCK):
            if q != p:
                factor = pivots[q][p]
                for c in range(p + 1, BLOCK):
                    pivots[q][c] = pivots[q][c] - factor * pivots[p][c]
                top[q] = top[q] - factor * top[p]
                side[q] = side[q] - factor * side[p]
    row = lax.broadcasted_iota(jnp.int32, left[0].shape, 0)
    last_left, last_right = top[0], side[0]
    for p in range(1, BLOCK):
        last_left = jnp.where(row == p, top[p], last_left)
        last_right = jnp.where(row == p, side[p], last_right)
    next_left, next_right = [], []
    for t in range(1, len(left)):
        a, b = left[t], right[t]
        for q in range(BLOCK):
            a = a - cols[t][q] * top[q]
            b = b - cols[t][q] * side[q]
        next_left.append(a)
        next_right.append(b)
    next_left.append(last_left)
    next_right.append(last_right)
    turn = left[0].shape[1] - BLOCK
    return [pltpu.roll(a, turn, 1) for a in next_left], next_right


def solve_kernel(total_ref, out_ref):
    n = out_ref.shape[0]
    row = lax.broadcasted_iota(jnp.int32, (n, n), 0)
    column = lax.broadcasted_iota(jnp.int32, (n, n), 1)
    system = total_ref[:n] + jnp.where(row == column, n - 1.0, 0.0)
    right_side = total_ref[n:].T
    left = [system[t : t + BLOCK] for t in range(0, n, BLOCK)]
    right = [right_side[t : t + BLOCK] for t in range(0, n, BLOCK)]
    _, solved = lax.fori_loop(0, n // BLOCK, lambda _, lr: eliminate(*lr), (left, right))
    solved = jnp.concatenate(solved, axis=0)
    out_ref[...] = solved - jnp.mean(solved, axis=0, keepdims=True)


def centred_coefficients(total):
    n = total.shape[1]
    return pl.pallas_call(
        solve_kernel,
        out_shape=jax.ShapeDtypeStruct((n, n), jnp.float32),
        cost_estimate=pl.CostEstimate(flops=40000000, bytes_accessed=200000, transcendentals=0),
        compiler_params=pltpu.CompilerParams(vmem_limit_bytes=4 * 1024 * 1024),
    )(total)


def exchange(value, axes):
    return lax.all_to_all(value, axes, split_axis=0, concat_axis=0, tiled=True)


def spread_to(value, axes):
    count = lax.axis_size(axes)
    return exchange(jnp.broadcast_to(value[None], (count,) + value.shape), axes)


def total_of(partial):
    near = lax.axis_size(NEAR)
    piece = jnp.sum(exchange(partial.reshape(near, -1, partial.shape[1]), NEAR), axis=0)
    piece = jnp.sum(spread_to(piece, "z"), axis=0)
    return spread_to(piece, NEAR).reshape(partial.shape)


def on_device(
    states,
    batch_index,
    obs_pick,
    norm_gain,
    w_in,
    b_in,
    member_params,
    observed,
    perturbation,
    inv_sigma,
):
    members = lax.axis_size(MEM)
    width = w_in.shape[1]
    features = w_in.shape[0]
    step_count, rows = batch_index.shape
    picked = obs_pick.shape[1]
    own = member_params.reshape(-1, features)
    weights = lax.all_gather(own, "r", axis=0, tiled=True)
    param_block = exchange(own.reshape(members, -1, features), MEM)
    step_scale = DT * width ** (-0.5)
    current = states.astype(jnp.float32)
    for turn in range(2):
        if turn:
            current, param_block = lax.optimization_barrier((current, param_block))
        layer = hidden_layer(current, norm_gain, w_in, b_in)
        current = current + step_scale * jnp.dot(layer, weights, preferred_element_type=jnp.float32)
    feature_ids = lax.broadcasted_iota(jnp.int32, (step_count, features, picked), 1)
    selector = (feature_ids == obs_pick[:, None, :]).astype(jnp.float32)
    state_ids = lax.broadcasted_iota(jnp.int32, (step_count, rows, states.shape[0]), 2)
    row_selector = (state_ids == batch_index[:, :, None]).astype(jnp.float32)
    narrowed = jnp.einsum("bs,ksf->kbf", current, selector, precision=HIGHEST)
    predicted = jnp.einsum("kib,kbf->kif", row_selector, narrowed, precision=HIGHEST)
    scaled = predicted * inv_sigma
    weighted = scaled.astype(jnp.bfloat16)
    misfit_w = (
        observed.astype(jnp.float32) * inv_sigma + perturbation[0].astype(jnp.float32) - scaled
    ).astype(jnp.bfloat16)
    misfit_local = jnp.sum(jnp.square(misfit_w.astype(jnp.float32)))
    entries = members * step_count * rows * lax.axis_size("r") * picked
    sent = jnp.concatenate(
        [weighted.reshape(members, -1, picked), misfit_w.reshape(members, -1, picked)], axis=1
    )
    gathered, misfit_here = jnp.split(exchange(sent, MEM), 2, axis=1)
    gathered = gathered.astype(jnp.float32)
    anomaly = (gathered - jnp.mean(gathered, axis=0)).astype(jnp.bfloat16)
    both = jnp.concatenate([anomaly, misfit_here], axis=0)
    partial = lax.dot_general(
        both, anomaly, (((1, 2), (1, 2)), ((), ())), preferred_element_type=jnp.float32
    )
    unit = lax.broadcasted_iota(jnp.int32, partial.shape, 0) == lax.broadcasted_iota(
        jnp.int32, partial.shape, 1
    )
    partial = partial + jnp.where(unit, misfit_local * ((members - 1) / entries), 0.0)
    total = total_of(partial)
    centred = centred_coefficients(total)
    params_f = param_block.astype(jnp.float32)
    change = jnp.einsum("kj,kap->jap", centred, params_f, precision=HIGHEST)
    renewed = (params_f + change).astype(jnp.bfloat16)
    return exchange(renewed, MEM).reshape(member_params.shape)


def solution(mesh):
    fine = Mesh(mesh.devices.reshape(4, 16, 2, 4), ("x", "z", "c", "r"))
    placed = (
        P("r", None),
        P(None, "r"),
        P(),
        P(),
        P(),
        P(),
        P(OWNERS, "r"),
        P(None, "r", None),
        P(OWNERS, None, "r", None),
        P(None, "r", None),
    )
    return jax.shard_map(
        on_device, mesh=fine, in_specs=placed, out_specs=P(OWNERS, "r"), check_vma=False
    )
```

```python
import jax
import jax.numpy as jnp
from jax import lax
from jax.experimental import pallas as pl
from jax.experimental.pallas import tpu as pltpu
from jax.sharding import Mesh
from jax.sharding import PartitionSpec as P

EPS = 1e-06
DT = 0.5
MEM = ("z", "x", "c")
OWNERS = ("x", "z", "c")
NEAR = ("x", "c", "r")
BLOCK = 8
HIGHEST = lax.Precision.HIGHEST


def hidden_layer(state, norm_gain, w_in, b_in):
    normed = (
        state * lax.rsqrt(jnp.mean(state * state, axis=-1, keepdims=True) + EPS) * norm_gain
    ).astype(jnp.bfloat16)
    return jax.nn.gelu(jnp.dot(normed, w_in, preferred_element_type=jnp.float32) + b_in).astype(
        jnp.bfloat16
    )


def eliminate(left, right):
    wide = lambda v: jnp.broadcast_to(v, left[0].shape)
    cols = [[wide(tile[:, q : q + 1]) for q in range(BLOCK)] for tile in left]
    pivots = [[wide(cols[0][q][p : p + 1]) for q in range(BLOCK)] for p in range(BLOCK)]
    top = [wide(left[0][p : p + 1]) for p in range(BLOCK)]
    side = [wide(right[0][p : p + 1]) for p in range(BLOCK)]
    for p in range(BLOCK):
        inverse = 1.0 / pivots[p][p]
        for c in range(p + 1, BLOCK):
            pivots[p][c] = pivots[p][c] * inverse
        top[p] = top[p] * inverse
        side[p] = side[p] * inverse
        for q in range(BLOCK):
            if q != p:
                factor = pivots[q][p]
                for c in range(p + 1, BLOCK):
                    pivots[q][c] = pivots[q][c] - factor * pivots[p][c]
                top[q] = top[q] - factor * top[p]
                side[q] = side[q] - factor * side[p]
    row = lax.broadcasted_iota(jnp.int32, left[0].shape, 0)
    last_left, last_right = top[0], side[0]
    for p in range(1, BLOCK):
        last_left = jnp.where(row == p, top[p], last_left)
        last_right = jnp.where(row == p, side[p], last_right)
    next_left, next_right = [], []
    for t in range(1, len(left)):
        a, b = left[t], right[t]
        for q in range(BLOCK):
            a = a - cols[t][q] * top[q]
            b = b - cols[t][q] * side[q]
        next_left.append(a)
        next_right.append(b)
    next_left.append(last_left)
    next_right.append(last_right)
    turn = left[0].shape[1] - BLOCK
    return [pltpu.roll(a, turn, 1) for a in next_left], next_right


def solve_kernel(total_ref, out_ref):
    n = out_ref.shape[0]
    row = lax.broadcasted_iota(jnp.int32, (n, n), 0)
    column = lax.broadcasted_iota(jnp.int32, (n, n), 1)
    system = total_ref[:n] + jnp.where(row == column, n - 1.0, 0.0)
    right_side = total_ref[n:].T
    left = [system[t : t + BLOCK] for t in range(0, n, BLOCK)]
    right = [right_side[t : t + BLOCK] for t in range(0, n, BLOCK)]
    _, solved = lax.fori_loop(0, n // BLOCK, lambda _, lr: eliminate(*lr), (left, right))
    solved = jnp.concatenate(solved, axis=0)
    out_ref[...] = solved - jnp.mean(solved, axis=0, keepdims=True)


def centred_coefficients(total):
    n = total.shape[1]
    return pl.pallas_call(
        solve_kernel,
        out_shape=jax.ShapeDtypeStruct((n, n), jnp.float32),
        cost_estimate=pl.CostEstimate(flops=40000000, bytes_accessed=200000, transcendentals=0),
        compiler_params=pltpu.CompilerParams(vmem_limit_bytes=4 * 1024 * 1024),
    )(total)


def exchange(value, axes):
    return lax.all_to_all(value, axes, split_axis=0, concat_axis=0, tiled=True)


def spread_to(value, axes):
    count = lax.axis_size(axes)
    return exchange(jnp.broadcast_to(value[None], (count,) + value.shape), axes)


def total_of(partial):
    near = lax.axis_size(NEAR)
    piece = jnp.sum(exchange(partial.reshape(near, -1, partial.shape[1]), NEAR), axis=0)
    piece = jnp.sum(spread_to(piece, "z"), axis=0)
    return spread_to(piece, NEAR).reshape(partial.shape)


def on_device(
    states,
    batch_index,
    obs_pick,
    norm_gain,
    w_in,
    b_in,
    member_params,
    observed,
    perturbation,
    inv_sigma,
):
    members = lax.axis_size(MEM)
    width = w_in.shape[1]
    features = w_in.shape[0]
    step_count, rows = batch_index.shape
    picked = obs_pick.shape[1]
    own = member_params.reshape(-1, features)
    ring = lax.axis_size("r")
    blocks = [own]
    for d in (1, 3, 2):
        blocks.insert(
            len(blocks) if d != 2 else 2,
            lax.ppermute(own, "r", [((i + d) % ring, i) for i in range(ring)]),
        )
    weights = jnp.concatenate(blocks, axis=0)
    turned = lax.axis_index("r") * own.shape[0]
    w_in = lax.dynamic_slice_in_dim(jnp.concatenate([w_in, w_in], axis=1), turned, width, 1)
    b_in = lax.dynamic_slice_in_dim(jnp.concatenate([b_in, b_in]), turned, width, 0)
    param_block = exchange(own.reshape(members, -1, features), MEM)
    step_scale = DT * width ** (-0.5)
    current = states.astype(jnp.float32)
    for turn in range(2):
        if turn:
            current, param_block = lax.optimization_barrier((current, param_block))
        layer = hidden_layer(current, norm_gain, w_in, b_in)
        current = current + step_scale * jnp.dot(layer, weights, preferred_element_type=jnp.float32)
    feature_ids = lax.broadcasted_iota(jnp.int32, (step_count, features, picked), 1)
    selector = (feature_ids == obs_pick[:, None, :]).astype(jnp.float32)
    state_ids = lax.broadcasted_iota(jnp.int32, (step_count, rows, states.shape[0]), 2)
    row_selector = (state_ids == batch_index[:, :, None]).astype(jnp.float32)
    narrowed = jnp.einsum("bs,ksf->kbf", current, selector, precision=HIGHEST)
    predicted = jnp.einsum("kib,kbf->kif", row_selector, narrowed, precision=HIGHEST)
    scaled = predicted * inv_sigma
    weighted = scaled.astype(jnp.bfloat16)
    misfit_w = (
        observed.astype(jnp.float32) * inv_sigma + perturbation[0].astype(jnp.float32) - scaled
    ).astype(jnp.bfloat16)
    misfit_local = jnp.sum(jnp.square(misfit_w.astype(jnp.float32)))
    entries = members * step_count * rows * lax.axis_size("r") * picked
    sent = jnp.concatenate(
        [weighted.reshape(members, -1, picked), misfit_w.reshape(members, -1, picked)], axis=1
    )
    gathered, misfit_here = jnp.split(exchange(sent, MEM), 2, axis=1)
    gathered = gathered.astype(jnp.float32)
    anomaly = (gathered - jnp.mean(gathered, axis=0)).astype(jnp.bfloat16)
    both = jnp.concatenate([anomaly, misfit_here], axis=0)
    partial = lax.dot_general(
        both, anomaly, (((1, 2), (1, 2)), ((), ())), preferred_element_type=jnp.float32
    )
    unit = lax.broadcasted_iota(jnp.int32, partial.shape, 0) == lax.broadcasted_iota(
        jnp.int32, partial.shape, 1
    )
    partial = partial + jnp.where(unit, misfit_local * ((members - 1) / entries), 0.0)
    total = total_of(partial)
    centred = centred_coefficients(total)
    params_f = param_block.astype(jnp.float32)
    change = jnp.einsum("kj,kap->jap", centred, params_f, precision=HIGHEST)
    renewed = (params_f + change).astype(jnp.bfloat16)
    return exchange(renewed, MEM).reshape(member_params.shape)


def solution(mesh):
    fine = Mesh(mesh.devices.reshape(4, 16, 2, 4), ("x", "z", "c", "r"))
    placed = (
        P("r", None),
        P(None, "r"),
        P(),
        P(),
        P(),
        P(),
        P(OWNERS, "r"),
        P(None, "r", None),
        P(OWNERS, None, "r", None),
        P(None, "r", None),
    )
    return jax.shard_map(
        on_device, mesh=fine, in_specs=placed, out_specs=P(OWNERS, "r"), check_vma=False
    )
```

```python
import jax
import jax.numpy as jnp
from jax import lax
from jax.experimental import pallas as pl
from jax.experimental.pallas import tpu as pltpu
from jax.sharding import Mesh
from jax.sharding import PartitionSpec as P

EPS = 1e-06
DT = 0.5
MEM = ("z", "x", "c")
OWNERS = ("x", "z", "c")
NEAR = ("x", "c", "r")
BLOCK = 8
HIGHEST = lax.Precision.HIGHEST


def hidden_layer(state, norm_gain, w_in, b_in):
    normed = (
        state * lax.rsqrt(jnp.mean(state * state, axis=-1, keepdims=True) + EPS) * norm_gain
    ).astype(jnp.bfloat16)
    return jax.nn.gelu(jnp.dot(normed, w_in, preferred_element_type=jnp.float32) + b_in).astype(
        jnp.bfloat16
    )


def eliminate(left, right):
    wide = lambda v: jnp.broadcast_to(v, left[0].shape)
    cols = [[wide(tile[:, q : q + 1]) for q in range(BLOCK)] for tile in left]
    pivots = [[wide(cols[0][q][p : p + 1]) for q in range(BLOCK)] for p in range(BLOCK)]
    top = [wide(left[0][p : p + 1]) for p in range(BLOCK)]
    side = [wide(right[0][p : p + 1]) for p in range(BLOCK)]
    for p in range(BLOCK):
        inverse = 1.0 / pivots[p][p]
        for c in range(p + 1, BLOCK):
            pivots[p][c] = pivots[p][c] * inverse
        top[p] = top[p] * inverse
        side[p] = side[p] * inverse
        for q in range(BLOCK):
            if q != p:
                factor = pivots[q][p]
                for c in range(p + 1, BLOCK):
                    pivots[q][c] = pivots[q][c] - factor * pivots[p][c]
                top[q] = top[q] - factor * top[p]
                side[q] = side[q] - factor * side[p]
    row = lax.broadcasted_iota(jnp.int32, left[0].shape, 0)
    last_left, last_right = top[0], side[0]
    for p in range(1, BLOCK):
        last_left = jnp.where(row == p, top[p], last_left)
        last_right = jnp.where(row == p, side[p], last_right)
    next_left, next_right = [], []
    for t in range(1, len(left)):
        a, b = left[t], right[t]
        for q in range(BLOCK):
            a = a - cols[t][q] * top[q]
            b = b - cols[t][q] * side[q]
        next_left.append(a)
        next_right.append(b)
    next_left.append(last_left)
    next_right.append(last_right)
    turn = left[0].shape[1] - BLOCK
    return [pltpu.roll(a, turn, 1) for a in next_left], next_right


def solve_kernel(total_ref, out_ref):
    n = out_ref.shape[0]
    row = lax.broadcasted_iota(jnp.int32, (n, n), 0)
    column = lax.broadcasted_iota(jnp.int32, (n, n), 1)
    system = total_ref[:n] + jnp.where(row == column, n - 1.0, 0.0)
    right_side = total_ref[n:].T
    left = [system[t : t + BLOCK] for t in range(0, n, BLOCK)]
    right = [right_side[t : t + BLOCK] for t in range(0, n, BLOCK)]
    _, solved = lax.fori_loop(0, n // BLOCK, lambda _, lr: eliminate(*lr), (left, right))
    solved = jnp.concatenate(solved, axis=0)
    out_ref[...] = solved - jnp.mean(solved, axis=0, keepdims=True)


def centred_coefficients(total):
    n = total.shape[1]
    return pl.pallas_call(
        solve_kernel,
        out_shape=jax.ShapeDtypeStruct((n, n), jnp.float32),
        cost_estimate=pl.CostEstimate(flops=40000000, bytes_accessed=200000, transcendentals=0),
        compiler_params=pltpu.CompilerParams(vmem_limit_bytes=4 * 1024 * 1024),
    )(total)


def exchange(value, axes):
    return lax.all_to_all(value, axes, split_axis=0, concat_axis=0, tiled=True)


def spread_to(value, axes):
    count = lax.axis_size(axes)
    return exchange(jnp.broadcast_to(value[None], (count,) + value.shape), axes)


def total_of(partial):
    near = lax.axis_size(NEAR)
    piece = jnp.sum(exchange(partial.reshape(near, -1, partial.shape[1]), NEAR), axis=0)
    piece = jnp.sum(spread_to(piece, "z"), axis=0)
    return spread_to(piece, NEAR).reshape(partial.shape)


def on_device(
    states,
    batch_index,
    obs_pick,
    norm_gain,
    w_in,
    b_in,
    member_params,
    observed,
    perturbation,
    inv_sigma,
):
    members = lax.axis_size(MEM)
    width = w_in.shape[1]
    features = w_in.shape[0]
    step_count, rows = batch_index.shape
    picked = obs_pick.shape[1]
    noise = exchange(perturbation.reshape(members, -1, picked), MEM)
    own = member_params.reshape(-1, features)
    weights = lax.all_gather(own, "r", axis=0, tiled=True)
    step_scale = DT * width ** (-0.5)
    current = states.astype(jnp.float32)
    for _ in range(2):
        layer = hidden_layer(current, norm_gain, w_in, b_in)
        current = current + step_scale * jnp.dot(layer, weights, preferred_element_type=jnp.float32)
    feature_ids = lax.broadcasted_iota(jnp.int32, (step_count, features, picked), 1)
    selector = (feature_ids == obs_pick[:, None, :]).astype(jnp.float32)
    state_ids = lax.broadcasted_iota(jnp.int32, (step_count, rows, states.shape[0]), 2)
    row_selector = (state_ids == batch_index[:, :, None]).astype(jnp.float32)
    narrowed = jnp.einsum("bs,ksf->kbf", current, selector, precision=HIGHEST)
    predicted = jnp.einsum("kib,kbf->kif", row_selector, narrowed, precision=HIGHEST)
    scaled = predicted * inv_sigma
    weighted = scaled.astype(jnp.bfloat16)
    misfit_w = (
        observed.astype(jnp.float32) * inv_sigma + perturbation[0].astype(jnp.float32) - scaled
    ).astype(jnp.bfloat16)
    misfit_local = jnp.sum(jnp.square(misfit_w.astype(jnp.float32)))
    entries = members * step_count * rows * lax.axis_size("r") * picked
    pairs = (members, -1, 2, picked)
    sent = jnp.concatenate([weighted.reshape(pairs), own.reshape(pairs)], axis=1)
    sent, noise = lax.optimization_barrier((sent, noise))
    arrived = exchange(sent, MEM)
    noise = noise.reshape(pairs)
    depth = noise.shape[1]
    gathered = arrived[:, :depth].astype(jnp.float32)
    param_block = arrived[:, depth:]
    place = lax.axis_index(MEM) * (2 * depth)
    aim = lax.dynamic_slice_in_dim(
        observed.reshape(-1, picked), place, 2 * depth, 0
    ).astype(jnp.float32) * lax.dynamic_slice_in_dim(
        inv_sigma.reshape(-1, picked), place, 2 * depth, 0
    )
    anomaly = (gathered - jnp.mean(gathered, axis=0)).astype(jnp.bfloat16)
    misfit_here = (
        aim.reshape(depth, 2, picked) + noise.astype(jnp.float32) - gathered
    ).astype(jnp.bfloat16)
    both = jnp.concatenate([anomaly, misfit_here], axis=0)
    partial = lax.dot_general(
        both, anomaly, (((1, 2, 3), (1, 2, 3)), ((), ())), preferred_element_type=jnp.float32
    )
    unit = lax.broadcasted_iota(jnp.int32, partial.shape, 0) == lax.broadcasted_iota(
        jnp.int32, partial.shape, 1
    )
    partial = partial + jnp.where(unit, misfit_local * ((members - 1) / entries), 0.0)
    total = total_of(partial)
    centred = centred_coefficients(total)
    params_f = param_block.astype(jnp.float32)
    change = jnp.einsum("kj,kabp->jabp", centred, params_f, precision=HIGHEST)
    renewed = (params_f + change).astype(jnp.bfloat16)
    return exchange(renewed, MEM).reshape(member_params.shape)


def solution(mesh):
    fine = Mesh(mesh.devices.reshape(4, 16, 2, 4), ("x", "z", "c", "r"))
    placed = (
        P("r", None),
        P(None, "r"),
        P(),
        P(),
        P(),
        P(),
        P(OWNERS, "r"),
        P(None, "r", None),
        P(OWNERS, None, "r", None),
        P(None, "r", None),
    )
    return jax.shard_map(
        on_device, mesh=fine, in_specs=placed, out_specs=P(OWNERS, "r"), check_vma=False
    )
```

```python
import jax
import jax.numpy as jnp
from jax import lax
from jax.experimental import pallas as pl
from jax.experimental.pallas import tpu as pltpu
from jax.sharding import Mesh
from jax.sharding import PartitionSpec as P

EPS = 1e-06
DT = 0.5
MEM = ("z", "x", "c")
OWNERS = ("x", "z", "c")
NEAR = ("x", "c", "r")
BLOCK = 8
HIGHEST = lax.Precision.HIGHEST


def hidden_layer(state, norm_gain, w_in, b_in):
    normed = (
        state * lax.rsqrt(jnp.mean(state * state, axis=-1, keepdims=True) + EPS) * norm_gain
    ).astype(jnp.bfloat16)
    return jax.nn.gelu(jnp.dot(normed, w_in, preferred_element_type=jnp.float32) + b_in).astype(
        jnp.bfloat16
    )


def eliminate(left, right):
    wide = lambda v: jnp.broadcast_to(v, left[0].shape)
    cols = [[wide(tile[:, q : q + 1]) for q in range(BLOCK)] for tile in left]
    pivots = [[wide(cols[0][q][p : p + 1]) for q in range(BLOCK)] for p in range(BLOCK)]
    top = [wide(left[0][p : p + 1]) for p in range(BLOCK)]
    side = [wide(right[0][p : p + 1]) for p in range(BLOCK)]
    for p in range(BLOCK):
        inverse = 1.0 / pivots[p][p]
        for c in range(p + 1, BLOCK):
            pivots[p][c] = pivots[p][c] * inverse
        top[p] = top[p] * inverse
        side[p] = side[p] * inverse
        for q in range(BLOCK):
            if q != p:
                factor = pivots[q][p]
                for c in range(p + 1, BLOCK):
                    pivots[q][c] = pivots[q][c] - factor * pivots[p][c]
                top[q] = top[q] - factor * top[p]
                side[q] = side[q] - factor * side[p]
    row = lax.broadcasted_iota(jnp.int32, left[0].shape, 0)
    last_left, last_right = top[0], side[0]
    for p in range(1, BLOCK):
        last_left = jnp.where(row == p, top[p], last_left)
        last_right = jnp.where(row == p, side[p], last_right)
    next_left, next_right = [], []
    for t in range(1, len(left)):
        a, b = left[t], right[t]
        for q in range(BLOCK):
            a = a - cols[t][q] * top[q]
            b = b - cols[t][q] * side[q]
        next_left.append(a)
        next_right.append(b)
    next_left.append(last_left)
    next_right.append(last_right)
    turn = left[0].shape[1] - BLOCK
    return [pltpu.roll(a, turn, 1) for a in next_left], next_right


def solve_kernel(total_ref, out_ref):
    n = out_ref.shape[0]
    row = lax.broadcasted_iota(jnp.int32, (n, n), 0)
    column = lax.broadcasted_iota(jnp.int32, (n, n), 1)
    system = total_ref[:n] + jnp.where(row == column, n - 1.0, 0.0)
    right_side = total_ref[n:].T
    left = [system[t : t + BLOCK] for t in range(0, n, BLOCK)]
    right = [right_side[t : t + BLOCK] for t in range(0, n, BLOCK)]
    _, solved = lax.fori_loop(0, n // BLOCK, lambda _, lr: eliminate(*lr), (left, right))
    solved = jnp.concatenate(solved, axis=0)
    out_ref[...] = solved - jnp.mean(solved, axis=0, keepdims=True)


def centred_coefficients(total):
    n = total.shape[1]
    return pl.pallas_call(
        solve_kernel,
        out_shape=jax.ShapeDtypeStruct((n, n), jnp.float32),
        cost_estimate=pl.CostEstimate(flops=40000000, bytes_accessed=200000, transcendentals=0),
        compiler_params=pltpu.CompilerParams(vmem_limit_bytes=4 * 1024 * 1024),
    )(total)


def exchange(value, axes):
    return lax.all_to_all(value, axes, split_axis=0, concat_axis=0, tiled=True)


def spread_to(value, axes):
    count = lax.axis_size(axes)
    return exchange(jnp.broadcast_to(value[None], (count,) + value.shape), axes)


def total_of(partial):
    near = lax.axis_size(NEAR)
    piece = jnp.sum(exchange(partial.reshape(near, -1, partial.shape[1]), NEAR), axis=0)
    piece = jnp.sum(spread_to(piece, "z"), axis=0)
    return spread_to(piece, NEAR).reshape(partial.shape)


def on_device(
    states,
    batch_index,
    obs_pick,
    norm_gain,
    w_in,
    b_in,
    member_params,
    observed,
    perturbation,
    inv_sigma,
):
    members = lax.axis_size(MEM)
    width = w_in.shape[1]
    features = w_in.shape[0]
    step_count, rows = batch_index.shape
    picked = obs_pick.shape[1]
    own = member_params.reshape(-1, features)
    weights = lax.all_gather(own, "r", axis=0, tiled=True)
    step_scale = DT * width ** (-0.5)
    current = states.astype(jnp.float32)
    for _ in range(2):
        layer = hidden_layer(current, norm_gain, w_in, b_in)
        current = current + step_scale * jnp.dot(layer, weights, preferred_element_type=jnp.float32)
    feature_ids = lax.broadcasted_iota(jnp.int32, (step_count, features, picked), 1)
    selector = (feature_ids == obs_pick[:, None, :]).astype(jnp.float32)
    state_ids = lax.broadcasted_iota(jnp.int32, (step_count, rows, states.shape[0]), 2)
    row_selector = (state_ids == batch_index[:, :, None]).astype(jnp.float32)
    narrowed = jnp.einsum("bs,ksf->kbf", current, selector, precision=HIGHEST)
    predicted = jnp.einsum("kib,kbf->kif", row_selector, narrowed, precision=HIGHEST)
    scaled = predicted * inv_sigma
    weighted = scaled.astype(jnp.bfloat16)
    misfit_w = (
        observed.astype(jnp.float32) * inv_sigma + perturbation[0].astype(jnp.float32) - scaled
    ).astype(jnp.bfloat16)
    misfit_local = jnp.sum(jnp.square(misfit_w.astype(jnp.float32)))
    entries = members * step_count * rows * lax.axis_size("r") * picked
    pairs = (members, -1, 2, picked)
    pairs = (members, -1, 2, picked)
    sent = [weighted.reshape(pairs), misfit_w.reshape(pairs), own.reshape(pairs)]
    depth = sent[0].shape[1]
    arrived = exchange(jnp.concatenate(sent, axis=1), MEM)
    gathered = arrived[:, :depth].astype(jnp.float32)
    misfit_here = arrived[:, depth : 2 * depth]
    param_block = arrived[:, 2 * depth :]
    anomaly = (gathered - jnp.mean(gathered, axis=0)).astype(jnp.bfloat16)
    both = jnp.concatenate([anomaly, misfit_here], axis=0)
    partial = lax.dot_general(
        both, anomaly, (((1, 2, 3), (1, 2, 3)), ((), ())), preferred_element_type=jnp.float32
    )
    unit = lax.broadcasted_iota(jnp.int32, partial.shape, 0) == lax.broadcasted_iota(
        jnp.int32, partial.shape, 1
    )
    partial = partial + jnp.where(unit, misfit_local * ((members - 1) / entries), 0.0)
    total = total_of(partial)
    centred = centred_coefficients(total)
    params_f = param_block.astype(jnp.float32)
    change = jnp.einsum("kj,kabp->jabp", centred, params_f, precision=HIGHEST)
    renewed = (params_f + change).astype(jnp.bfloat16)
    return exchange(renewed, MEM).reshape(member_params.shape)


def solution(mesh):
    fine = Mesh(mesh.devices.reshape(4, 16, 2, 4), ("x", "z", "c", "r"))
    placed = (
        P("r", None),
        P(None, "r"),
        P(),
        P(),
        P(),
        P(),
        P(OWNERS, "r"),
        P(None, "r", None),
        P(OWNERS, None, "r", None),
        P(None, "r", None),
    )
    return jax.shard_map(
        on_device, mesh=fine, in_specs=placed, out_specs=P(OWNERS, "r"), check_vma=False
    )
```

```python
import jax
import jax.numpy as jnp
from jax import lax
from jax.experimental import pallas as pl
from jax.experimental.pallas import tpu as pltpu
from jax.sharding import Mesh
from jax.sharding import PartitionSpec as P

EPS = 1e-06
DT = 0.5
MEM = ("z", "x", "c")
OWNERS = ("x", "z", "c")
NEAR = ("x", "c", "r")
BLOCK = 8
HIGHEST = lax.Precision.HIGHEST


def hidden_layer(state, norm_gain, w_in, b_in):
    normed = (
        state * lax.rsqrt(jnp.mean(state * state, axis=-1, keepdims=True) + EPS) * norm_gain
    ).astype(jnp.bfloat16)
    return jax.nn.gelu(jnp.dot(normed, w_in, preferred_element_type=jnp.float32) + b_in).astype(
        jnp.bfloat16
    )


def eliminate(left, right):
    wide = lambda v: jnp.broadcast_to(v, left[0].shape)
    cols = [[wide(tile[:, q : q + 1]) for q in range(BLOCK)] for tile in left]
    pivots = [[wide(cols[0][q][p : p + 1]) for q in range(p + 1)] for p in range(BLOCK)]
    top = [wide(left[0][p : p + 1]) for p in range(BLOCK)]
    side = [wide(right[0][p : p + 1]) for p in range(BLOCK)]
    factors = {}
    for p in range(BLOCK):
        inverse = 1.0 / pivots[p][p]
        for q in range(p + 1, BLOCK):
            factors[q, p] = factor = pivots[q][p] * inverse
            for c in range(p + 1, q + 1):
                pivots[q][c] = pivots[q][c] - factor * pivots[c][p]
            top[q] = top[q] - factor * top[p]
            side[q] = side[q] - factor * side[p]
        top[p] = top[p] * inverse
        side[p] = side[p] * inverse
    for p in reversed(range(BLOCK)):
        for q in range(p):
            top[q] = top[q] - factors[p, q] * top[p]
            side[q] = side[q] - factors[p, q] * side[p]
    row = lax.broadcasted_iota(jnp.int32, left[0].shape, 0)
    last_left, last_right = top[0], side[0]
    for p in range(1, BLOCK):
        last_left = jnp.where(row == p, top[p], last_left)
        last_right = jnp.where(row == p, side[p], last_right)
    next_left, next_right = [], []
    for t in range(1, len(left)):
        a, b = left[t], right[t]
        for q in range(BLOCK):
            a = a - cols[t][q] * top[q]
            b = b - cols[t][q] * side[q]
        next_left.append(a)
        next_right.append(b)
    next_left.append(last_left)
    next_right.append(last_right)
    turn = left[0].shape[1] - BLOCK
    return [pltpu.roll(a, turn, 1) for a in next_left], next_right


def solve_kernel(total_ref, out_ref):
    n = out_ref.shape[0]
    row = lax.broadcasted_iota(jnp.int32, (n, n), 0)
    column = lax.broadcasted_iota(jnp.int32, (n, n), 1)
    system = total_ref[:n] + jnp.where(row == column, n - 1.0, 0.0)
    right_side = total_ref[n:].T
    left = [system[t : t + BLOCK] for t in range(0, n, BLOCK)]
    right = [right_side[t : t + BLOCK] for t in range(0, n, BLOCK)]
    _, solved = lax.fori_loop(0, n // BLOCK, lambda _, lr: eliminate(*lr), (left, right))
    solved = jnp.concatenate(solved, axis=0)
    out_ref[...] = solved - jnp.mean(solved, axis=0, keepdims=True)


def centred_coefficients(total):
    n = total.shape[1]
    return pl.pallas_call(
        solve_kernel,
        out_shape=jax.ShapeDtypeStruct((n, n), jnp.float32),
        cost_estimate=pl.CostEstimate(flops=40000000, bytes_accessed=200000, transcendentals=0),
        compiler_params=pltpu.CompilerParams(vmem_limit_bytes=4 * 1024 * 1024),
    )(total)


def exchange(value, axes):
    return lax.all_to_all(value, axes, split_axis=0, concat_axis=0, tiled=True)


def spread_to(value, axes):
    count = lax.axis_size(axes)
    return exchange(jnp.broadcast_to(value[None], (count,) + value.shape), axes)


def total_of(partial):
    near = lax.axis_size(NEAR)
    piece = jnp.sum(exchange(partial.reshape(near, -1, partial.shape[1]), NEAR), axis=0)
    piece = jnp.sum(spread_to(piece, "z"), axis=0)
    return spread_to(piece, NEAR).reshape(partial.shape)


def on_device(
    states,
    batch_index,
    obs_pick,
    norm_gain,
    w_in,
    b_in,
    member_params,
    observed,
    perturbation,
    inv_sigma,
):
    members = lax.axis_size(MEM)
    width = w_in.shape[1]
    features = w_in.shape[0]
    step_count, rows = batch_index.shape
    picked = obs_pick.shape[1]
    own = member_params.reshape(-1, features)
    weights = lax.all_gather(own, "r", axis=0, tiled=True)
    step_scale = DT * width ** (-0.5)
    current = states.astype(jnp.float32)
    for _ in range(2):
        layer = hidden_layer(current, norm_gain, w_in, b_in)
        current = current + step_scale * jnp.dot(layer, weights, preferred_element_type=jnp.float32)
    feature_ids = lax.broadcasted_iota(jnp.int32, (step_count, features, picked), 1)
    selector = (feature_ids == obs_pick[:, None, :]).astype(jnp.float32)
    state_ids = lax.broadcasted_iota(jnp.int32, (step_count, rows, states.shape[0]), 2)
    row_selector = (state_ids == batch_index[:, :, None]).astype(jnp.float32)
    narrowed = jnp.einsum("bs,ksf->kbf", current, selector, precision=HIGHEST)
    predicted = jnp.einsum("kib,kbf->kif", row_selector, narrowed, precision=HIGHEST)
    scaled = predicted * inv_sigma
    weighted = scaled.astype(jnp.bfloat16)
    misfit_w = (
        observed.astype(jnp.float32) * inv_sigma + perturbation[0].astype(jnp.float32) - scaled
    ).astype(jnp.bfloat16)
    misfit_local = jnp.sum(jnp.square(misfit_w.astype(jnp.float32)))
    entries = members * step_count * rows * lax.axis_size("r") * picked
    pairs = (members, -1, 2, picked)
    pairs = (members, -1, 2, picked)
    sent = [weighted.reshape(pairs), misfit_w.reshape(pairs), own.reshape(pairs)]
    depth = sent[0].shape[1]
    arrived = exchange(jnp.concatenate(sent, axis=1), MEM)
    gathered = arrived[:, :depth].astype(jnp.float32)
    misfit_here = arrived[:, depth : 2 * depth]
    param_block = arrived[:, 2 * depth :]
    param_block, gathered = lax.optimization_barrier((param_block, gathered))
    anomaly = (gathered - jnp.mean(gathered, axis=0)).astype(jnp.bfloat16)
    both = jnp.concatenate([anomaly, misfit_here], axis=0)
    partial = lax.dot_general(
        both, anomaly, (((1, 2, 3), (1, 2, 3)), ((), ())), preferred_element_type=jnp.float32
    )
    unit = lax.broadcasted_iota(jnp.int32, partial.shape, 0) == lax.broadcasted_iota(
        jnp.int32, partial.shape, 1
    )
    partial = partial + jnp.where(unit, misfit_local * ((members - 1) / entries), 0.0)
    total = total_of(partial)
    centred = centred_coefficients(total)
    params_f = param_block.astype(jnp.float32)
    change = jnp.einsum("kj,kabp->jabp", centred, params_f, precision=HIGHEST)
    renewed = (params_f + change).astype(jnp.bfloat16)
    return exchange(renewed, MEM).reshape(member_params.shape)


def solution(mesh):
    fine = Mesh(mesh.devices.reshape(4, 16, 2, 4), ("x", "z", "c", "r"))
    placed = (
        P("r", None),
        P(None, "r"),
        P(),
        P(),
        P(),
        P(),
        P(OWNERS, "r"),
        P(None, "r", None),
        P(OWNERS, None, "r", None),
        P(None, "r", None),
    )
    return jax.shard_map(
        on_device, mesh=fine, in_specs=placed, out_specs=P(OWNERS, "r"), check_vma=False
    )
```

```python
import jax
import jax.numpy as jnp
from jax import lax
from jax.experimental import pallas as pl
from jax.experimental.pallas import tpu as pltpu
from jax.sharding import Mesh
from jax.sharding import PartitionSpec as P

EPS = 1e-06
DT = 0.5
MEM = ("z", "x", "c")
OWNERS = ("x", "z", "c")
NEAR = ("x", "c", "r")
BLOCK = 8
LANES = 128
HIGHEST = lax.Precision.HIGHEST


def hidden_layer(state, norm_gain, w_in, b_in):
    normed = (
        state * lax.rsqrt(jnp.mean(state * state, axis=-1, keepdims=True) + EPS) * norm_gain
    ).astype(jnp.bfloat16)
    return jax.nn.gelu(jnp.dot(normed, w_in, preferred_element_type=jnp.float32) + b_in).astype(
        jnp.bfloat16
    )


def wide(value):
    return jnp.broadcast_to(value, (BLOCK, value.shape[1] if value.shape[1] > 1 else LANES))


def split(value):
    head = value.astype(jnp.bfloat16).astype(jnp.float32)
    rest = value - head
    middle = rest.astype(jnp.bfloat16).astype(jnp.float32)
    return head, middle, rest - middle


def pivot_rows(left, right):
    cols = [wide(left[:, q : q + 1]) for q in range(BLOCK)]
    pivots = [[wide(cols[q][p : p + 1]) for q in range(p + 1)] for p in range(BLOCK)]
    top = [wide(left[p : p + 1]) for p in range(BLOCK)]
    side = [wide(right[p : p + 1]) for p in range(BLOCK)]
    factors = {}
    for p in range(0, BLOCK, 2):
        a, b, d = pivots[p][p], pivots[p + 1][p], pivots[p + 1][p + 1]
        inverse = 1.0 / (a * d - b * b)
        ia, ib, id_ = d * inverse, -(b * inverse), a * inverse
        for q in range(p + 2, BLOCK):
            factors[q, p] = f = pivots[q][p] * ia + pivots[q][p + 1] * ib
            factors[q, p + 1] = g = pivots[q][p] * ib + pivots[q][p + 1] * id_
            for c in range(p + 2, q + 1):
                pivots[q][c] = pivots[q][c] - f * pivots[c][p] - g * pivots[c][p + 1]
            top[q] = top[q] - f * top[p] - g * top[p + 1]
            side[q] = side[q] - f * side[p] - g * side[p + 1]
        for rows in (top, side):
            rows[p], rows[p + 1] = ia * rows[p] + ib * rows[p + 1], ib * rows[p] + id_ * rows[p + 1]
    for p in reversed(range(2, BLOCK)):
        for q in range(p // 2 * 2):
            top[q] = top[q] - factors[p, q] * top[p]
            side[q] = side[q] - factors[p, q] * side[p]
    row = lax.broadcasted_iota(jnp.int32, left.shape, 0)
    tile, side_tile = top[0], side[0]
    for p in range(1, BLOCK):
        tile = jnp.where(row == p, top[p], tile)
        side_tile = jnp.where(row == p, side[p], side_tile)
    return tile, side_tile, top, side


def eliminate(left, right, tile, side_tile):
    n = left.shape[0]
    tile, side_tile, top, side = pivot_rows(tile, side_tile)
    near, near_side = left[BLOCK : 2 * BLOCK], right[BLOCK : 2 * BLOCK]
    cols = [wide(near[:, q : q + 1]) for q in range(BLOCK)]
    for q in range(BLOCK):
        near = near - cols[q] * top[q]
        near_side = near_side - cols[q] * side[q]
    column = lax.broadcasted_iota(jnp.int32, left.shape, 1)
    a, b, c = split(jnp.where(column < BLOCK, left, 0.0))
    factor = a
    for place, part in enumerate((a, a, b, b, c)):
        factor = factor + pltpu.roll(part, (place + 1) * BLOCK, 1)
    a, b, c = split(jnp.concatenate([tile, side_tile], axis=1))
    unused = jnp.zeros((n - 6 * BLOCK, 2 * n), jnp.float32)
    rows = jnp.concatenate([a, b, c, a, b, a, unused], axis=0)
    change = jnp.dot(
        factor.astype(jnp.bfloat16), rows.astype(jnp.bfloat16), preferred_element_type=jnp.float32
    )
    left = jnp.concatenate([(left - change[:, :n])[BLOCK:], tile], axis=0)
    right = jnp.concatenate([(right - change[:, n:])[BLOCK:], side_tile], axis=0)
    return pltpu.roll(left, n - BLOCK, 1), right, pltpu.roll(near, n - BLOCK, 1), near_side


def solve_kernel(total_ref, out_ref):
    n = out_ref.shape[0]
    row = lax.broadcasted_iota(jnp.int32, (n, n), 0)
    column = lax.broadcasted_iota(jnp.int32, (n, n), 1)
    left = total_ref[:n] + jnp.where(row == column, n - 1.0, 0.0)
    right = total_ref[n:].T
    state = (left, right, left[:BLOCK], right[:BLOCK])
    for _ in range(n // BLOCK):
        state = eliminate(*state)
    solved = state[1]
    out_ref[...] = solved - jnp.mean(solved, axis=0, keepdims=True)


def centred_coefficients(total):
    n = total.shape[1]
    return pl.pallas_call(
        solve_kernel,
        out_shape=jax.ShapeDtypeStruct((n, n), jnp.float32),
        cost_estimate=pl.CostEstimate(flops=40000000, bytes_accessed=200000, transcendentals=0),
        compiler_params=pltpu.CompilerParams(vmem_limit_bytes=8 * 1024 * 1024),
    )(total)


def exchange(value, axes):
    return lax.all_to_all(value, axes, split_axis=0, concat_axis=0, tiled=True)


def spread_to(value, axes):
    count = lax.axis_size(axes)
    return exchange(jnp.broadcast_to(value[None], (count,) + value.shape), axes)


def total_of(partial):
    near = lax.axis_size(NEAR)
    piece = jnp.sum(exchange(partial.reshape(near, -1, partial.shape[1]), NEAR), axis=0)
    piece = jnp.sum(spread_to(piece, "z"), axis=0)
    return spread_to(piece, NEAR).reshape(partial.shape)


def on_device(
    states,
    batch_index,
    obs_pick,
    norm_gain,
    w_in,
    b_in,
    member_params,
    observed,
    perturbation,
    inv_sigma,
):
    members = lax.axis_size(MEM)
    width = w_in.shape[1]
    features = w_in.shape[0]
    step_count, rows = batch_index.shape
    picked = obs_pick.shape[1]
    own = member_params.reshape(-1, features)
    weights = lax.all_gather(own, "r", axis=0, tiled=True)
    step_scale = DT * width ** (-0.5)
    current = states.astype(jnp.float32)
    for _ in range(2):
        layer = hidden_layer(current, norm_gain, w_in, b_in)
        current = current + step_scale * jnp.dot(layer, weights, preferred_element_type=jnp.float32)
    feature_ids = lax.broadcasted_iota(jnp.int32, (step_count, features, picked), 1)
    selector = (feature_ids == obs_pick[:, None, :]).astype(jnp.float32)
    state_ids = lax.broadcasted_iota(jnp.int32, (step_count, rows, states.shape[0]), 2)
    row_selector = (state_ids == batch_index[:, :, None]).astype(jnp.float32)
    narrowed = jnp.einsum("bs,ksf->kbf", current, selector, precision=HIGHEST)
    predicted = jnp.einsum("kib,kbf->kif", row_selector, narrowed, precision=HIGHEST)
    scaled = predicted * inv_sigma
    weighted = scaled.astype(jnp.bfloat16)
    misfit_w = (
        observed.astype(jnp.float32) * inv_sigma + perturbation[0].astype(jnp.float32) - scaled
    ).astype(jnp.bfloat16)
    misfit_local = jnp.sum(jnp.square(misfit_w.astype(jnp.float32)))
    entries = members * step_count * rows * lax.axis_size("r") * picked
    pairs = (members, -1, 2, picked)
    pairs = (members, -1, 2, picked)
    depth = step_count * rows // members // 2
    sent = lax.pad(
        own.reshape(pairs), jnp.bfloat16(0), ((0, 0, 0), (2 * depth, 0, 0), (0, 0, 0), (0, 0, 0))
    )
    sent = lax.dynamic_update_slice(sent, weighted.reshape(pairs), (0, 0, 0, 0))
    sent = lax.dynamic_update_slice(sent, misfit_w.reshape(pairs), (0, depth, 0, 0))
    arrived = exchange(sent, MEM)
    gathered = arrived[:, :depth].astype(jnp.float32)
    misfit_here = arrived[:, depth : 2 * depth]
    param_block = arrived[:, 2 * depth :]
    param_block, gathered = lax.optimization_barrier((param_block, gathered))
    anomaly = (gathered - jnp.mean(gathered, axis=0)).astype(jnp.bfloat16)
    both = jnp.concatenate([anomaly, misfit_here], axis=0)
    partial = lax.dot_general(
        both, anomaly, (((1, 2, 3), (1, 2, 3)), ((), ())), preferred_element_type=jnp.float32
    )
    unit = lax.broadcasted_iota(jnp.int32, partial.shape, 0) == lax.broadcasted_iota(
        jnp.int32, partial.shape, 1
    )
    partial = partial + jnp.where(unit, misfit_local * ((members - 1) / entries), 0.0)
    total = total_of(partial)
    centred = centred_coefficients(total)
    params_f = param_block.astype(jnp.float32)
    change = jnp.einsum("kj,kabp->jabp", centred, params_f, precision=HIGHEST)
    renewed = (params_f + change).astype(jnp.bfloat16)
    return exchange(renewed, MEM).reshape(member_params.shape)


def solution(mesh):
    fine = Mesh(mesh.devices.reshape(4, 16, 2, 4), ("x", "z", "c", "r"))
    placed = (
        P("r", None),
        P(None, "r"),
        P(),
        P(),
        P(),
        P(),
        P(OWNERS, "r"),
        P(None, "r", None),
        P(OWNERS, None, "r", None),
        P(None, "r", None),
    )
    return jax.shard_map(
        on_device, mesh=fine, in_specs=placed, out_specs=P(OWNERS, "r"), check_vma=False
    )
```

```python
import jax
import jax.numpy as jnp
from jax import lax
from jax.experimental import pallas as pl
from jax.experimental.pallas import tpu as pltpu
from jax.sharding import Mesh
from jax.sharding import PartitionSpec as P

EPS = 1e-06
DT = 0.5
MEM = ("z", "x", "c")
OWNERS = ("x", "z", "c")
NEAR = ("x", "c", "r")
BLOCK = 8
LANES = 128
HIGHEST = lax.Precision.HIGHEST


def hidden_layer(state, norm_gain, w_in, b_in):
    normed = (
        state * lax.rsqrt(jnp.mean(state * state, axis=-1, keepdims=True) + EPS) * norm_gain
    ).astype(jnp.bfloat16)
    return jax.nn.gelu(jnp.dot(normed, w_in, preferred_element_type=jnp.float32) + b_in).astype(
        jnp.bfloat16
    )


def wide(value):
    return jnp.broadcast_to(value, (BLOCK, value.shape[1] if value.shape[1] > 1 else LANES))


def split(value):
    head = value.astype(jnp.bfloat16).astype(jnp.float32)
    rest = value - head
    middle = rest.astype(jnp.bfloat16).astype(jnp.float32)
    return head, middle, rest - middle


def pivot_rows(left, right):
    cols = [wide(left[:, q : q + 1]) for q in range(BLOCK)]
    pivots = [[wide(cols[q][p : p + 1]) for q in range(p + 1)] for p in range(BLOCK)]
    top = [wide(left[p : p + 1]) for p in range(BLOCK)]
    side = [wide(right[p : p + 1]) for p in range(BLOCK)]
    factors = {}
    for p in range(0, BLOCK, 2):
        a, b, d = pivots[p][p], pivots[p + 1][p], pivots[p + 1][p + 1]
        inverse = 1.0 / (a * d - b * b)
        ia, ib, id_ = d * inverse, -(b * inverse), a * inverse
        for q in range(p + 2, BLOCK):
            factors[q, p] = f = pivots[q][p] * ia + pivots[q][p + 1] * ib
            factors[q, p + 1] = g = pivots[q][p] * ib + pivots[q][p + 1] * id_
            for c in range(p + 2, q + 1):
                pivots[q][c] = pivots[q][c] - f * pivots[c][p] - g * pivots[c][p + 1]
            top[q] = top[q] - f * top[p] - g * top[p + 1]
            side[q] = side[q] - f * side[p] - g * side[p + 1]
        for rows in (top, side):
            rows[p], rows[p + 1] = ia * rows[p] + ib * rows[p + 1], ib * rows[p] + id_ * rows[p + 1]
    for p in reversed(range(2, BLOCK)):
        for q in range(p // 2 * 2):
            top[q] = top[q] - factors[p, q] * top[p]
            side[q] = side[q] - factors[p, q] * side[p]
    row = lax.broadcasted_iota(jnp.int32, left.shape, 0)
    tile, side_tile = top[0], side[0]
    for p in range(1, BLOCK):
        tile = jnp.where(row == p, top[p], tile)
        side_tile = jnp.where(row == p, side[p], side_tile)
    return tile, side_tile, top, side


def eliminate(left, right, tile, side_tile):
    n = left.shape[0]
    tile, side_tile, top, side = pivot_rows(tile, side_tile)
    near, near_side = left[BLOCK : 2 * BLOCK], right[BLOCK : 2 * BLOCK]
    cols = [wide(near[:, q : q + 1]) for q in range(BLOCK)]
    for q in range(BLOCK):
        near = near - cols[q] * top[q]
        near_side = near_side - cols[q] * side[q]
    column = lax.broadcasted_iota(jnp.int32, left.shape, 1)
    a, b, c = split(jnp.where(column < BLOCK, left, 0.0))
    factor = a
    for place, part in enumerate((a, a, b, b, c)):
        factor = factor + pltpu.roll(part, (place + 1) * BLOCK, 1)
    a, b, c = split(jnp.concatenate([tile, side_tile], axis=1))
    unused = jnp.zeros((n - 6 * BLOCK, 2 * n), jnp.float32)
    rows = jnp.concatenate([a, b, c, a, b, a, unused], axis=0)
    change = jnp.dot(
        factor.astype(jnp.bfloat16), rows.astype(jnp.bfloat16), preferred_element_type=jnp.float32
    )
    left = jnp.concatenate([(left - change[:, :n])[BLOCK:], tile], axis=0)
    right = jnp.concatenate([(right - change[:, n:])[BLOCK:], side_tile], axis=0)
    return pltpu.roll(left, n - BLOCK, 1), right, pltpu.roll(near, n - BLOCK, 1), near_side


def solve_kernel(total_ref, out_ref):
    n = out_ref.shape[0]
    row = lax.broadcasted_iota(jnp.int32, (n, n), 0)
    column = lax.broadcasted_iota(jnp.int32, (n, n), 1)
    left = total_ref[:n] + jnp.where(row == column, n - 1.0, 0.0)
    right = total_ref[n:].T
    state = (left, right, left[:BLOCK], right[:BLOCK])
    for _ in range(n // BLOCK):
        state = eliminate(*state)
    solved = state[1]
    out_ref[...] = solved - jnp.mean(solved, axis=0, keepdims=True)


def centred_coefficients(total):
    n = total.shape[1]
    return pl.pallas_call(
        solve_kernel,
        out_shape=jax.ShapeDtypeStruct((n, n), jnp.float32),
        cost_estimate=pl.CostEstimate(flops=40000000, bytes_accessed=200000, transcendentals=0),
        compiler_params=pltpu.CompilerParams(vmem_limit_bytes=8 * 1024 * 1024),
    )(total)


def exchange(value, axes):
    return lax.all_to_all(value, axes, split_axis=0, concat_axis=0, tiled=True)


def spread_to(value, axes):
    count = lax.axis_size(axes)
    return exchange(jnp.broadcast_to(value[None], (count,) + value.shape), axes)


def total_of(partial):
    near = lax.axis_size(NEAR)
    piece = jnp.sum(exchange(partial.reshape(near, -1, partial.shape[1]), NEAR), axis=0)
    piece = jnp.sum(spread_to(piece, "z"), axis=0)
    return spread_to(piece, NEAR).reshape(partial.shape)


def on_device(
    states,
    batch_index,
    obs_pick,
    norm_gain,
    w_in,
    b_in,
    member_params,
    observed,
    perturbation,
    inv_sigma,
):
    members = lax.axis_size(MEM)
    width = w_in.shape[1]
    features = w_in.shape[0]
    step_count, rows = batch_index.shape
    picked = obs_pick.shape[1]
    own = member_params.reshape(-1, features)
    weights = lax.all_gather(own, "r", axis=0, tiled=True)
    step_scale = DT * width ** (-0.5)
    current = states.astype(jnp.float32)
    for _ in range(2):
        layer = hidden_layer(current, norm_gain, w_in, b_in)
        current = current + step_scale * jnp.dot(layer, weights, preferred_element_type=jnp.float32)
    feature_ids = lax.broadcasted_iota(jnp.int32, (step_count, features, picked), 1)
    selector = (feature_ids == obs_pick[:, None, :]).astype(jnp.float32)
    state_ids = lax.broadcasted_iota(jnp.int32, (step_count, rows, states.shape[0]), 2)
    row_selector = (state_ids == batch_index[:, :, None]).astype(jnp.float32)
    narrowed = jnp.einsum("bs,ksf->kbf", current, selector, precision=HIGHEST)
    predicted = jnp.einsum("kib,kbf->kif", row_selector, narrowed, precision=HIGHEST)
    scaled = predicted * inv_sigma
    weighted = scaled.astype(jnp.bfloat16)
    misfit_w = (
        observed.astype(jnp.float32) * inv_sigma + perturbation[0].astype(jnp.float32) - scaled
    ).astype(jnp.bfloat16)
    misfit_local = jnp.sum(jnp.square(misfit_w.astype(jnp.float32)))
    entries = members * step_count * rows * lax.axis_size("r") * picked
    pairs = (members, -1, 2, picked)
    pairs = (members, -1, 2, picked)
    sent = [weighted.reshape(pairs), misfit_w.reshape(pairs), own.reshape(pairs)]
    depth = sent[0].shape[1]
    misfit_share = misfit_local * ((members - 1) / entries)
    sent, misfit_share = lax.optimization_barrier((jnp.concatenate(sent, axis=1), misfit_share))
    arrived = exchange(sent, MEM)
    gathered = arrived[:, :depth].astype(jnp.float32)
    misfit_here = arrived[:, depth : 2 * depth]
    param_block = arrived[:, 2 * depth :]
    param_block, gathered = lax.optimization_barrier((param_block, gathered))
    anomaly = (gathered - jnp.mean(gathered, axis=0)).astype(jnp.bfloat16)
    both = jnp.concatenate([anomaly, misfit_here], axis=0)
    partial = lax.dot_general(
        both, anomaly, (((1, 2, 3), (1, 2, 3)), ((), ())), preferred_element_type=jnp.float32
    )
    unit = lax.broadcasted_iota(jnp.int32, partial.shape, 0) == lax.broadcasted_iota(
        jnp.int32, partial.shape, 1
    )
    partial = partial + jnp.where(unit, misfit_share, 0.0)
    total = total_of(partial)
    centred = centred_coefficients(total)
    params_f = param_block.astype(jnp.float32)
    change = jnp.einsum("kj,kabp->jabp", centred, params_f, precision=HIGHEST)
    renewed = (params_f + change).astype(jnp.bfloat16)
    return exchange(renewed, MEM).reshape(member_params.shape)


def solution(mesh):
    fine = Mesh(mesh.devices.reshape(4, 16, 2, 4), ("x", "z", "c", "r"))
    placed = (
        P("r", None),
        P(None, "r"),
        P(),
        P(),
        P(),
        P(),
        P(OWNERS, "r"),
        P(None, "r", None),
        P(OWNERS, None, "r", None),
        P(None, "r", None),
    )
    return jax.shard_map(
        on_device, mesh=fine, in_specs=placed, out_specs=P(OWNERS, "r"), check_vma=False
    )
```

```python
import jax
import jax.numpy as jnp
from jax import lax
from jax.experimental import pallas as pl
from jax.experimental.pallas import tpu as pltpu
from jax.sharding import Mesh
from jax.sharding import PartitionSpec as P

EPS = 1e-06
DT = 0.5
MEM = ("z", "x", "c")
OWNERS = ("x", "z", "c")
NEAR = ("x", "c", "r")
BLOCK = 8
LANES = 128
HIGHEST = lax.Precision.HIGHEST


def hidden_layer(state, norm_gain, w_in, b_in):
    normed = (
        state * lax.rsqrt(jnp.mean(state * state, axis=-1, keepdims=True) + EPS) * norm_gain
    ).astype(jnp.bfloat16)
    return jax.nn.gelu(jnp.dot(normed, w_in, preferred_element_type=jnp.float32) + b_in).astype(
        jnp.bfloat16
    )


def wide(value):
    return jnp.broadcast_to(value, (BLOCK, value.shape[1] if value.shape[1] > 1 else LANES))


def split(value):
    head = value.astype(jnp.bfloat16).astype(jnp.float32)
    rest = value - head
    middle = rest.astype(jnp.bfloat16).astype(jnp.float32)
    return head, middle, rest - middle


def pivot_rows(left, right):
    cols = [wide(left[:, q : q + 1]) for q in range(BLOCK)]
    pivots = [[wide(cols[q][p : p + 1]) for q in range(p + 1)] for p in range(BLOCK)]
    top = [wide(left[p : p + 1]) for p in range(BLOCK)]
    side = [wide(right[p : p + 1]) for p in range(BLOCK)]
    factors = {}
    for p in range(0, BLOCK, 2):
        a, b, d = pivots[p][p], pivots[p + 1][p], pivots[p + 1][p + 1]
        inverse = 1.0 / (a * d - b * b)
        ia, ib, id_ = d * inverse, -(b * inverse), a * inverse
        for q in range(p + 2, BLOCK):
            factors[q, p] = f = pivots[q][p] * ia + pivots[q][p + 1] * ib
            factors[q, p + 1] = g = pivots[q][p] * ib + pivots[q][p + 1] * id_
            for c in range(p + 2, q + 1):
                pivots[q][c] = pivots[q][c] - f * pivots[c][p] - g * pivots[c][p + 1]
            top[q] = top[q] - f * top[p] - g * top[p + 1]
            side[q] = side[q] - f * side[p] - g * side[p + 1]
        for rows in (top, side):
            rows[p], rows[p + 1] = ia * rows[p] + ib * rows[p + 1], ib * rows[p] + id_ * rows[p + 1]
    for p in reversed(range(2, BLOCK)):
        for q in range(p // 2 * 2):
            top[q] = top[q] - factors[p, q] * top[p]
            side[q] = side[q] - factors[p, q] * side[p]
    row = lax.broadcasted_iota(jnp.int32, left.shape, 0)
    tile, side_tile = top[0], side[0]
    for p in range(1, BLOCK):
        tile = jnp.where(row == p, top[p], tile)
        side_tile = jnp.where(row == p, side[p], side_tile)
    return tile, side_tile, top, side


def eliminate(left, right, tile, side_tile):
    n = left.shape[0]
    tile, side_tile, top, side = pivot_rows(tile, side_tile)
    near, near_side = left[BLOCK : 2 * BLOCK], right[BLOCK : 2 * BLOCK]
    cols = [wide(near[:, q : q + 1]) for q in range(BLOCK)]
    for q in range(BLOCK):
        near = near - cols[q] * top[q]
        near_side = near_side - cols[q] * side[q]
    column = lax.broadcasted_iota(jnp.int32, left.shape, 1)
    a, b, c = split(jnp.where(column < BLOCK, left, 0.0))
    factor = a
    for place, part in enumerate((a, a, b, b, c)):
        factor = factor + pltpu.roll(part, (place + 1) * BLOCK, 1)
    a, b, c = split(jnp.concatenate([tile, side_tile], axis=1))
    unused = jnp.zeros((n - 6 * BLOCK, 2 * n), jnp.float32)
    rows = jnp.concatenate([a, b, c, a, b, a, unused], axis=0)
    change = jnp.dot(
        factor.astype(jnp.bfloat16), rows.astype(jnp.bfloat16), preferred_element_type=jnp.float32
    )
    left = jnp.concatenate([(left - change[:, :n])[BLOCK:], tile], axis=0)
    right = jnp.concatenate([(right - change[:, n:])[BLOCK:], side_tile], axis=0)
    return pltpu.roll(left, n - BLOCK, 1), right, pltpu.roll(near, n - BLOCK, 1), near_side


def solve_kernel(total_ref, out_ref):
    n = out_ref.shape[0]
    row = lax.broadcasted_iota(jnp.int32, (n, n), 0)
    column = lax.broadcasted_iota(jnp.int32, (n, n), 1)
    left = total_ref[:n] + jnp.where(row == column, n - 1.0, 0.0)
    right = total_ref[n:].T
    state = (left, right, left[:BLOCK], right[:BLOCK])
    for _ in range(n // BLOCK):
        state = eliminate(*state)
    solved = state[1]
    out_ref[...] = solved - jnp.mean(solved, axis=0, keepdims=True)


def centred_coefficients(total):
    n = total.shape[1]
    return pl.pallas_call(
        solve_kernel,
        out_shape=jax.ShapeDtypeStruct((n, n), jnp.float32),
        cost_estimate=pl.CostEstimate(flops=40000000, bytes_accessed=200000, transcendentals=0),
        compiler_params=pltpu.CompilerParams(vmem_limit_bytes=8 * 1024 * 1024),
    )(total)


def relayout_kernel(row_ref, out_ref):
    out_ref[...] = row_ref[...].reshape(out_ref.shape)


def lane_rows(row):
    return pl.pallas_call(
        relayout_kernel,
        out_shape=jax.ShapeDtypeStruct((row.shape[1] // LANES, LANES), row.dtype),
        cost_estimate=pl.CostEstimate(flops=0, bytes_accessed=4 * row.size, transcendentals=0),
        compiler_params=pltpu.CompilerParams(vmem_limit_bytes=4 * 1024 * 1024),
    )(row)


def exchange(value, axes):
    return lax.all_to_all(value, axes, split_axis=0, concat_axis=0, tiled=True)


def spread_to(value, axes):
    count = lax.axis_size(axes)
    return exchange(jnp.broadcast_to(value[None], (count,) + value.shape), axes)


def total_of(partial):
    near = lax.axis_size(NEAR)
    piece = jnp.sum(exchange(partial.reshape(near, -1, partial.shape[1]), NEAR), axis=0)
    piece = jnp.sum(spread_to(piece, "z"), axis=0)
    return spread_to(piece, NEAR).reshape(partial.shape)


def on_device(
    states,
    batch_index,
    obs_pick,
    norm_gain,
    w_in,
    b_in,
    member_params,
    observed,
    perturbation,
    inv_sigma,
):
    members = lax.axis_size(MEM)
    width = w_in.shape[1]
    features = w_in.shape[0]
    step_count, rows = batch_index.shape
    picked = obs_pick.shape[1]
    own = lane_rows(member_params).reshape(-1, features)
    weights = lax.all_gather(own, "r", axis=0, tiled=True)
    step_scale = DT * width ** (-0.5)
    current = states.astype(jnp.float32)
    for _ in range(2):
        layer = hidden_layer(current, norm_gain, w_in, b_in)
        current = current + step_scale * jnp.dot(layer, weights, preferred_element_type=jnp.float32)
    feature_ids = lax.broadcasted_iota(jnp.int32, (step_count, features, picked), 1)
    selector = (feature_ids == obs_pick[:, None, :]).astype(jnp.float32)
    state_ids = lax.broadcasted_iota(jnp.int32, (step_count, rows, states.shape[0]), 2)
    row_selector = (state_ids == batch_index[:, :, None]).astype(jnp.float32)
    narrowed = jnp.einsum("bs,ksf->kbf", current, selector, precision=HIGHEST)
    predicted = jnp.einsum("kib,kbf->kif", row_selector, narrowed, precision=HIGHEST)
    scaled = predicted * inv_sigma
    weighted = scaled.astype(jnp.bfloat16)
    misfit_w = (
        observed.astype(jnp.float32) * inv_sigma + perturbation[0].astype(jnp.float32) - scaled
    ).astype(jnp.bfloat16)
    misfit_local = jnp.sum(jnp.square(misfit_w.astype(jnp.float32)))
    entries = members * step_count * rows * lax.axis_size("r") * picked
    pairs = (members, -1, 2, picked)
    pairs = (members, -1, 2, picked)
    sent = [weighted.reshape(pairs), misfit_w.reshape(pairs), own.reshape(pairs)]
    depth = sent[0].shape[1]
    arrived = exchange(jnp.concatenate(sent, axis=1), MEM)
    gathered = arrived[:, :depth].astype(jnp.float32)
    misfit_here = arrived[:, depth : 2 * depth]
    param_block = arrived[:, 2 * depth :]
    param_block, gathered = lax.optimization_barrier((param_block, gathered))
    anomaly = (gathered - jnp.mean(gathered, axis=0)).astype(jnp.bfloat16)
    both = jnp.concatenate([anomaly, misfit_here], axis=0)
    partial = lax.dot_general(
        both, anomaly, (((1, 2, 3), (1, 2, 3)), ((), ())), preferred_element_type=jnp.float32
    )
    unit = lax.broadcasted_iota(jnp.int32, partial.shape, 0) == lax.broadcasted_iota(
        jnp.int32, partial.shape, 1
    )
    partial = partial + jnp.where(unit, (members - 1) / entries, 0.0) * misfit_local
    total = total_of(partial)
    centred = centred_coefficients(total)
    params_f = param_block.astype(jnp.float32)
    change = jnp.einsum("kj,kabp->jabp", centred, params_f, precision=HIGHEST)
    renewed = (params_f + change).astype(jnp.bfloat16)
    return exchange(renewed, MEM).reshape(member_params.shape)


def solution(mesh):
    fine = Mesh(mesh.devices.reshape(4, 16, 2, 4), ("x", "z", "c", "r"))
    placed = (
        P("r", None),
        P(None, "r"),
        P(),
        P(),
        P(),
        P(),
        P(OWNERS, "r"),
        P(None, "r", None),
        P(OWNERS, None, "r", None),
        P(None, "r", None),
    )
    return jax.shard_map(
        on_device, mesh=fine, in_specs=placed, out_specs=P(OWNERS, "r"), check_vma=False
    )
```

```python
import jax
import jax.numpy as jnp
from jax import lax
from jax.experimental import pallas as pl
from jax.experimental.pallas import tpu as pltpu
from jax.sharding import Mesh
from jax.sharding import PartitionSpec as P

EPS = 1e-06
DT = 0.5
MEM = ("z", "x", "c")
OWNERS = ("x", "z", "c")
NEAR = ("x", "c", "r")
BLOCK = 8
LANES = 128
HIGHEST = lax.Precision.HIGHEST


def hidden_layer(state, norm_gain, w_in, b_in):
    normed = (
        state * lax.rsqrt(jnp.mean(state * state, axis=-1, keepdims=True) + EPS) * norm_gain
    ).astype(jnp.bfloat16)
    return jax.nn.gelu(jnp.dot(normed, w_in, preferred_element_type=jnp.float32) + b_in).astype(
        jnp.bfloat16
    )


def wide(value):
    return jnp.broadcast_to(value, (BLOCK, value.shape[1] if value.shape[1] > 1 else LANES))


def split(value):
    head = value.astype(jnp.bfloat16).astype(jnp.float32)
    rest = value - head
    middle = rest.astype(jnp.bfloat16).astype(jnp.float32)
    return head, middle, rest - middle


def pivot_rows(left, right):
    cols = [wide(left[:, q : q + 1]) for q in range(BLOCK)]
    pivots = [[wide(cols[q][p : p + 1]) for q in range(p + 1)] for p in range(BLOCK)]
    top = [wide(left[p : p + 1]) for p in range(BLOCK)]
    side = [wide(right[p : p + 1]) for p in range(BLOCK)]
    factors = {}
    for p in range(0, BLOCK, 2):
        a, b, d = pivots[p][p], pivots[p + 1][p], pivots[p + 1][p + 1]
        inverse = 1.0 / (a * d - b * b)
        ia, ib, id_ = d * inverse, -(b * inverse), a * inverse
        for q in range(p + 2, BLOCK):
            factors[q, p] = f = pivots[q][p] * ia + pivots[q][p + 1] * ib
            factors[q, p + 1] = g = pivots[q][p] * ib + pivots[q][p + 1] * id_
            for c in range(p + 2, q + 1):
                pivots[q][c] = pivots[q][c] - f * pivots[c][p] - g * pivots[c][p + 1]
            top[q] = top[q] - f * top[p] - g * top[p + 1]
            side[q] = side[q] - f * side[p] - g * side[p + 1]
        for rows in (top, side):
            rows[p], rows[p + 1] = ia * rows[p] + ib * rows[p + 1], ib * rows[p] + id_ * rows[p + 1]
    for p in reversed(range(2, BLOCK)):
        for q in range(p // 2 * 2):
            top[q] = top[q] - factors[p, q] * top[p]
            side[q] = side[q] - factors[p, q] * side[p]
    row = lax.broadcasted_iota(jnp.int32, left.shape, 0)
    tile, side_tile = top[0], side[0]
    for p in range(1, BLOCK):
        tile = jnp.where(row == p, top[p], tile)
        side_tile = jnp.where(row == p, side[p], side_tile)
    return tile, side_tile, top, side


def eliminate(left, right, tile, side_tile):
    n = left.shape[0]
    tile, side_tile, top, side = pivot_rows(tile, side_tile)
    near, near_side = left[BLOCK : 2 * BLOCK], right[BLOCK : 2 * BLOCK]
    cols = [wide(near[:, q : q + 1]) for q in range(BLOCK)]
    for q in range(BLOCK):
        near = near - cols[q] * top[q]
        near_side = near_side - cols[q] * side[q]
    column = lax.broadcasted_iota(jnp.int32, left.shape, 1)
    a, b, c = split(jnp.where(column < BLOCK, left, 0.0))
    factor = a
    for place, part in enumerate((a, a, b, b, c)):
        factor = factor + pltpu.roll(part, (place + 1) * BLOCK, 1)
    a, b, c = split(jnp.concatenate([tile, side_tile], axis=1))
    unused = jnp.zeros((n - 6 * BLOCK, 2 * n), jnp.float32)
    rows = jnp.concatenate([a, b, c, a, b, a, unused], axis=0)
    change = jnp.dot(
        factor.astype(jnp.bfloat16), rows.astype(jnp.bfloat16), preferred_element_type=jnp.float32
    )
    left = jnp.concatenate([(left - change[:, :n])[BLOCK:], tile], axis=0)
    right = jnp.concatenate([(right - change[:, n:])[BLOCK:], side_tile], axis=0)
    return pltpu.roll(left, n - BLOCK, 1), right, pltpu.roll(near, n - BLOCK, 1), near_side


def solve_kernel(total_ref, out_ref):
    n = out_ref.shape[0]
    row = lax.broadcasted_iota(jnp.int32, (n, n), 0)
    column = lax.broadcasted_iota(jnp.int32, (n, n), 1)
    left = total_ref[:n] + jnp.where(row == column, n - 1.0, 0.0)
    right = total_ref[n:].T
    state = (left, right, left[:BLOCK], right[:BLOCK])
    for _ in range(n // BLOCK):
        state = eliminate(*state)
    solved = state[1]
    out_ref[...] = solved - jnp.mean(solved, axis=0, keepdims=True)


def centred_coefficients(total):
    n = total.shape[1]
    return pl.pallas_call(
        solve_kernel,
        out_shape=jax.ShapeDtypeStruct((n, n), jnp.float32),
        cost_estimate=pl.CostEstimate(flops=40000000, bytes_accessed=200000, transcendentals=0),
        compiler_params=pltpu.CompilerParams(vmem_limit_bytes=8 * 1024 * 1024),
    )(total)


def relayout_kernel(row_ref, out_ref):
    out_ref[...] = row_ref[...].reshape(out_ref.shape)


def lane_rows(row):
    return pl.pallas_call(
        relayout_kernel,
        out_shape=jax.ShapeDtypeStruct((row.shape[1] // LANES, LANES), row.dtype),
        cost_estimate=pl.CostEstimate(flops=0, bytes_accessed=4 * row.size, transcendentals=0),
        compiler_params=pltpu.CompilerParams(vmem_limit_bytes=4 * 1024 * 1024),
    )(row)


def exchange(value, axes):
    return lax.all_to_all(value, axes, split_axis=0, concat_axis=0, tiled=True)


def spread_to(value, axes):
    count = lax.axis_size(axes)
    return exchange(jnp.broadcast_to(value[None], (count,) + value.shape), axes)


def total_of(partial):
    near = lax.axis_size(NEAR)
    piece = jnp.sum(exchange(partial.reshape(near, -1, partial.shape[1]), NEAR), axis=0)
    piece = jnp.sum(spread_to(piece, "z"), axis=0)
    return spread_to(piece, NEAR).reshape(partial.shape)


def on_device(
    states,
    batch_index,
    obs_pick,
    norm_gain,
    w_in,
    b_in,
    member_params,
    observed,
    perturbation,
    inv_sigma,
):
    members = lax.axis_size(MEM)
    width = w_in.shape[1]
    features = w_in.shape[0]
    step_count, rows = batch_index.shape
    picked = obs_pick.shape[1]
    own = lane_rows(member_params).reshape(-1, features)
    weights = lax.all_gather(own, "r", axis=0, tiled=True)
    weights, states = lax.optimization_barrier((weights, states))
    step_scale = DT * width ** (-0.5)
    current = states.astype(jnp.float32)
    for _ in range(2):
        layer = hidden_layer(current, norm_gain, w_in, b_in)
        current = current + step_scale * jnp.dot(layer, weights, preferred_element_type=jnp.float32)
    feature_ids = lax.broadcasted_iota(jnp.int32, (step_count, features, picked), 1)
    selector = (feature_ids == obs_pick[:, None, :]).astype(jnp.float32)
    state_ids = lax.broadcasted_iota(jnp.int32, (step_count, rows, states.shape[0]), 2)
    row_selector = (state_ids == batch_index[:, :, None]).astype(jnp.float32)
    narrowed = jnp.einsum("bs,ksf->kbf", current, selector, precision=HIGHEST)
    predicted = jnp.einsum("kib,kbf->kif", row_selector, narrowed, precision=HIGHEST)
    scaled = predicted * inv_sigma
    weighted = scaled.astype(jnp.bfloat16)
    misfit_w = (
        observed.astype(jnp.float32) * inv_sigma + perturbation[0].astype(jnp.float32) - scaled
    ).astype(jnp.bfloat16)
    misfit_local = jnp.sum(jnp.square(misfit_w.astype(jnp.float32)))
    entries = members * step_count * rows * lax.axis_size("r") * picked
    pairs = (members, -1, 2, picked)
    pairs = (members, -1, 2, picked)
    sent = [weighted.reshape(pairs), misfit_w.reshape(pairs), own.reshape(pairs)]
    depth = sent[0].shape[1]
    arrived = exchange(jnp.concatenate(sent, axis=1), MEM)
    gathered = arrived[:, :depth].astype(jnp.float32)
    misfit_here = arrived[:, depth : 2 * depth]
    param_block = arrived[:, 2 * depth :]
    param_block, gathered = lax.optimization_barrier((param_block, gathered))
    anomaly = (gathered - jnp.mean(gathered, axis=0)).astype(jnp.bfloat16)
    both = jnp.concatenate([anomaly, misfit_here], axis=0)
    partial = lax.dot_general(
        both, anomaly, (((1, 2, 3), (1, 2, 3)), ((), ())), preferred_element_type=jnp.float32
    )
    unit = lax.broadcasted_iota(jnp.int32, partial.shape, 0) == lax.broadcasted_iota(
        jnp.int32, partial.shape, 1
    )
    partial = partial + jnp.where(unit, (members - 1) / entries, 0.0) * misfit_local
    total = total_of(partial)
    centred = centred_coefficients(total)
    params_f = param_block.astype(jnp.float32)
    change = jnp.einsum("kj,kabp->jabp", centred, params_f, precision=HIGHEST)
    renewed = (params_f + change).astype(jnp.bfloat16)
    return exchange(renewed, MEM).reshape(member_params.shape)


def solution(mesh):
    fine = Mesh(mesh.devices.reshape(4, 16, 2, 4), ("x", "z", "c", "r"))
    placed = (
        P("r", None),
        P(None, "r"),
        P(),
        P(),
        P(),
        P(),
        P(OWNERS, "r"),
        P(None, "r", None),
        P(OWNERS, None, "r", None),
        P(None, "r", None),
    )
    return jax.shard_map(
        on_device, mesh=fine, in_specs=placed, out_specs=P(OWNERS, "r"), check_vma=False
    )
```

```python
import jax
import jax.numpy as jnp
from jax import lax
from jax.experimental import pallas as pl
from jax.experimental.pallas import tpu as pltpu
from jax.sharding import Mesh
from jax.sharding import PartitionSpec as P

EPS = 1e-06
DT = 0.5
MEM = ("z", "x", "c")
OWNERS = ("x", "z", "c")
NEAR = ("x", "r", "c")
BLOCK = 8
LANES = 128
HIGHEST = lax.Precision.HIGHEST


def hidden_layer(state, norm_gain, w_in, b_in):
    normed = (
        state * lax.rsqrt(jnp.mean(state * state, axis=-1, keepdims=True) + EPS) * norm_gain
    ).astype(jnp.bfloat16)
    return jax.nn.gelu(jnp.dot(normed, w_in, preferred_element_type=jnp.float32) + b_in).astype(
        jnp.bfloat16
    )


def wide(value):
    return jnp.broadcast_to(value, (BLOCK, value.shape[1] if value.shape[1] > 1 else LANES))


def split(value):
    head = value.astype(jnp.bfloat16).astype(jnp.float32)
    rest = value - head
    middle = rest.astype(jnp.bfloat16).astype(jnp.float32)
    return head, middle, rest - middle


def pivot_rows(left, right):
    cols = [wide(left[:, q : q + 1]) for q in range(BLOCK)]
    pivots = [[wide(cols[q][p : p + 1]) for q in range(p + 1)] for p in range(BLOCK)]
    top = [wide(left[p : p + 1]) for p in range(BLOCK)]
    side = [wide(right[p : p + 1]) for p in range(BLOCK)]
    factors = {}
    for p in range(0, BLOCK, 2):
        a, b, d = pivots[p][p], pivots[p + 1][p], pivots[p + 1][p + 1]
        inverse = 1.0 / (a * d - b * b)
        ia, ib, id_ = d * inverse, -(b * inverse), a * inverse
        for q in range(p + 2, BLOCK):
            factors[q, p] = f = pivots[q][p] * ia + pivots[q][p + 1] * ib
            factors[q, p + 1] = g = pivots[q][p] * ib + pivots[q][p + 1] * id_
            for c in range(p + 2, q + 1):
                pivots[q][c] = pivots[q][c] - f * pivots[c][p] - g * pivots[c][p + 1]
            top[q] = top[q] - f * top[p] - g * top[p + 1]
            side[q] = side[q] - f * side[p] - g * side[p + 1]
        for rows in (top, side):
            rows[p], rows[p + 1] = ia * rows[p] + ib * rows[p + 1], ib * rows[p] + id_ * rows[p + 1]
    for p in reversed(range(2, BLOCK)):
        for q in range(p // 2 * 2):
            top[q] = top[q] - factors[p, q] * top[p]
            side[q] = side[q] - factors[p, q] * side[p]
    row = lax.broadcasted_iota(jnp.int32, left.shape, 0)
    tile, side_tile = top[0], side[0]
    for p in range(1, BLOCK):
        tile = jnp.where(row == p, top[p], tile)
        side_tile = jnp.where(row == p, side[p], side_tile)
    return tile, side_tile, top, side


def eliminate(left, right, tile, side_tile):
    n = left.shape[0]
    tile, side_tile, top, side = pivot_rows(tile, side_tile)
    near, near_side = left[BLOCK : 2 * BLOCK], right[BLOCK : 2 * BLOCK]
    cols = [wide(near[:, q : q + 1]) for q in range(BLOCK)]
    for q in range(BLOCK):
        near = near - cols[q] * top[q]
        near_side = near_side - cols[q] * side[q]
    column = lax.broadcasted_iota(jnp.int32, left.shape, 1)
    a, b, c = split(jnp.where(column < BLOCK, left, 0.0))
    factor = a
    for place, part in enumerate((a, a, b, b, c)):
        factor = factor + pltpu.roll(part, (place + 1) * BLOCK, 1)
    a, b, c = split(jnp.concatenate([tile, side_tile], axis=1))
    unused = jnp.zeros((n - 6 * BLOCK, 2 * n), jnp.float32)
    rows = jnp.concatenate([a, b, c, a, b, a, unused], axis=0)
    change = jnp.dot(
        factor.astype(jnp.bfloat16), rows.astype(jnp.bfloat16), preferred_element_type=jnp.float32
    )
    left = jnp.concatenate([(left - change[:, :n])[BLOCK:], tile], axis=0)
    right = jnp.concatenate([(right - change[:, n:])[BLOCK:], side_tile], axis=0)
    return pltpu.roll(left, n - BLOCK, 1), right, pltpu.roll(near, n - BLOCK, 1), near_side


def solve_kernel(total_ref, out_ref):
    n = out_ref.shape[0]
    row = lax.broadcasted_iota(jnp.int32, (n, n), 0)
    column = lax.broadcasted_iota(jnp.int32, (n, n), 1)
    left = total_ref[:n] + jnp.where(row == column, n - 1.0, 0.0)
    right = total_ref[n:].T
    state = (left, right, left[:BLOCK], right[:BLOCK])
    for _ in range(n // BLOCK):
        state = eliminate(*state)
    solved = state[1]
    out_ref[...] = solved - jnp.mean(solved, axis=0, keepdims=True)


def centred_coefficients(total):
    n = total.shape[1]
    return pl.pallas_call(
        solve_kernel,
        out_shape=jax.ShapeDtypeStruct((n, n), jnp.float32),
        cost_estimate=pl.CostEstimate(flops=40000000, bytes_accessed=200000, transcendentals=0),
        compiler_params=pltpu.CompilerParams(vmem_limit_bytes=8 * 1024 * 1024),
    )(total)


def relayout_kernel(row_ref, out_ref):
    out_ref[...] = row_ref[...].reshape(out_ref.shape)


def lane_rows(row):
    return pl.pallas_call(
        relayout_kernel,
        out_shape=jax.ShapeDtypeStruct((row.shape[1] // LANES, LANES), row.dtype),
        cost_estimate=pl.CostEstimate(flops=0, bytes_accessed=4 * row.size, transcendentals=0),
        compiler_params=pltpu.CompilerParams(vmem_limit_bytes=4 * 1024 * 1024),
    )(row)


def exchange(value, axes):
    return lax.all_to_all(value, axes, split_axis=0, concat_axis=0, tiled=True)


def spread_to(value, axes):
    count = lax.axis_size(axes)
    return exchange(jnp.broadcast_to(value[None], (count,) + value.shape), axes)


def total_of(partial):
    near = lax.axis_size(NEAR)
    piece = jnp.sum(exchange(partial.reshape(near, -1, partial.shape[1]), NEAR), axis=0)
    piece = jnp.sum(spread_to(piece, "z"), axis=0)
    return spread_to(piece, NEAR).reshape(partial.shape)


def on_device(
    states,
    batch_index,
    obs_pick,
    norm_gain,
    w_in,
    b_in,
    member_params,
    observed,
    perturbation,
    inv_sigma,
):
    members = lax.axis_size(MEM)
    width = w_in.shape[1]
    features = w_in.shape[0]
    step_count, rows = batch_index.shape
    picked = obs_pick.shape[1]
    own = lane_rows(member_params).reshape(-1, features)
    weights = lax.all_gather(own, "r", axis=0, tiled=True)
    weights, states = lax.optimization_barrier((weights, states))
    step_scale = DT * width ** (-0.5)
    current = states.astype(jnp.float32)
    for _ in range(2):
        layer = hidden_layer(current, norm_gain, w_in, b_in)
        current = current + step_scale * jnp.dot(layer, weights, preferred_element_type=jnp.float32)
    feature_ids = lax.broadcasted_iota(jnp.int32, (step_count, features, picked), 1)
    selector = (feature_ids == obs_pick[:, None, :]).astype(jnp.float32)
    state_ids = lax.broadcasted_iota(jnp.int32, (step_count, rows, states.shape[0]), 2)
    row_selector = (state_ids == batch_index[:, :, None]).astype(jnp.float32)
    narrowed = jnp.einsum("bs,ksf->kbf", current, selector, precision=HIGHEST)
    predicted = jnp.einsum("kib,kbf->kif", row_selector, narrowed, precision=HIGHEST)
    scaled = predicted * inv_sigma
    weighted = scaled.astype(jnp.bfloat16)
    misfit_w = (
        observed.astype(jnp.float32) * inv_sigma + perturbation[0].astype(jnp.float32) - scaled
    ).astype(jnp.bfloat16)
    misfit_local = jnp.sum(jnp.square(misfit_w.astype(jnp.float32)))
    entries = members * step_count * rows * lax.axis_size("r") * picked
    pairs = (members, -1, 2, picked)
    pairs = (members, -1, 2, picked)
    sent = [weighted.reshape(pairs), misfit_w.reshape(pairs), own.reshape(pairs)]
    depth = sent[0].shape[1]
    arrived = exchange(jnp.concatenate(sent, axis=1), MEM)
    gathered = arrived[:, :depth].astype(jnp.float32)
    misfit_here = arrived[:, depth : 2 * depth]
    param_block = arrived[:, 2 * depth :]
    param_block, gathered = lax.optimization_barrier((param_block, gathered))
    anomaly = (gathered - jnp.mean(gathered, axis=0)).astype(jnp.bfloat16)
    both = jnp.concatenate([anomaly, misfit_here], axis=0)
    partial = lax.dot_general(
        both, anomaly, (((1, 2, 3), (1, 2, 3)), ((), ())), preferred_element_type=jnp.float32
    )
    unit = lax.broadcasted_iota(jnp.int32, partial.shape, 0) == lax.broadcasted_iota(
        jnp.int32, partial.shape, 1
    )
    partial = partial + jnp.where(unit, (members - 1) / entries, 0.0) * misfit_local
    total = total_of(partial)
    centred = centred_coefficients(total)
    params_f = param_block.astype(jnp.float32)
    change = jnp.einsum("kj,kabp->jabp", centred, params_f, precision=HIGHEST)
    renewed = (params_f + change).astype(jnp.bfloat16)
    return exchange(renewed, MEM).reshape(member_params.shape)


def solution(mesh):
    fine = Mesh(mesh.devices.reshape(4, 16, 2, 4), ("x", "z", "c", "r"))
    placed = (
        P("r", None),
        P(None, "r"),
        P(),
        P(),
        P(),
        P(),
        P(OWNERS, "r"),
        P(None, "r", None),
        P(OWNERS, None, "r", None),
        P(None, "r", None),
    )
    return jax.shard_map(
        on_device, mesh=fine, in_specs=placed, out_specs=P(OWNERS, "r"), check_vma=False
    )
```

```python
import jax
import jax.numpy as jnp
from jax import lax
from jax.experimental import pallas as pl
from jax.experimental.pallas import tpu as pltpu
from jax.sharding import Mesh
from jax.sharding import PartitionSpec as P

EPS = 1e-06
DT = 0.5
MEM = ("z", "x", "c")
OWNERS = ("x", "z", "c")
NEAR = ("x", "c", "r")
BLOCK = 8
LANES = 128
HIGHEST = lax.Precision.HIGHEST


def hidden_layer(state, norm_gain, w_in, b_in):
    normed = (
        state * lax.rsqrt(jnp.mean(state * state, axis=-1, keepdims=True) + EPS) * norm_gain
    ).astype(jnp.bfloat16)
    return jax.nn.gelu(jnp.dot(normed, w_in, preferred_element_type=jnp.float32) + b_in).astype(
        jnp.bfloat16
    )


def wide(value):
    return jnp.broadcast_to(value, (BLOCK, value.shape[1] if value.shape[1] > 1 else LANES))


def split(value):
    head = value.astype(jnp.bfloat16).astype(jnp.float32)
    rest = value - head
    middle = rest.astype(jnp.bfloat16).astype(jnp.float32)
    return head, middle, rest - middle


def pivot_rows(left, right):
    cols = [wide(left[:, q : q + 1]) for q in range(BLOCK)]
    pivots = [[wide(cols[q][p : p + 1]) for q in range(p + 1)] for p in range(BLOCK)]
    top = [wide(left[p : p + 1]) for p in range(BLOCK)]
    side = [wide(right[p : p + 1]) for p in range(BLOCK)]
    factors = {}
    for p in range(0, BLOCK, 2):
        a, b, d = pivots[p][p], pivots[p + 1][p], pivots[p + 1][p + 1]
        inverse = 1.0 / (a * d - b * b)
        ia, ib, id_ = d * inverse, -(b * inverse), a * inverse
        for q in range(p + 2, BLOCK):
            factors[q, p] = f = pivots[q][p] * ia + pivots[q][p + 1] * ib
            factors[q, p + 1] = g = pivots[q][p] * ib + pivots[q][p + 1] * id_
            for c in range(p + 2, q + 1):
                pivots[q][c] = pivots[q][c] - f * pivots[c][p] - g * pivots[c][p + 1]
            top[q] = top[q] - f * top[p] - g * top[p + 1]
            side[q] = side[q] - f * side[p] - g * side[p + 1]
        for rows in (top, side):
            rows[p], rows[p + 1] = ia * rows[p] + ib * rows[p + 1], ib * rows[p] + id_ * rows[p + 1]
    for p in reversed(range(2, BLOCK)):
        for q in range(p // 2 * 2):
            top[q] = top[q] - factors[p, q] * top[p]
            side[q] = side[q] - factors[p, q] * side[p]
    row = lax.broadcasted_iota(jnp.int32, left.shape, 0)
    tile, side_tile = top[0], side[0]
    for p in range(1, BLOCK):
        tile = jnp.where(row == p, top[p], tile)
        side_tile = jnp.where(row == p, side[p], side_tile)
    return tile, side_tile, top, side


def eliminate(left, right, tile, side_tile):
    n = left.shape[0]
    tile, side_tile, top, side = pivot_rows(tile, side_tile)
    near, near_side = left[BLOCK : 2 * BLOCK], right[BLOCK : 2 * BLOCK]
    cols = [wide(near[:, q : q + 1]) for q in range(BLOCK)]
    for q in range(BLOCK):
        near = near - cols[q] * top[q]
        near_side = near_side - cols[q] * side[q]
    column = lax.broadcasted_iota(jnp.int32, left.shape, 1)
    a, b, c = split(jnp.where(column < BLOCK, left, 0.0))
    factor = a
    for place, part in enumerate((a, a, b, b, c)):
        factor = factor + pltpu.roll(part, (place + 1) * BLOCK, 1)
    a, b, c = split(jnp.concatenate([tile, side_tile], axis=1))
    unused = jnp.zeros((n - 6 * BLOCK, 2 * n), jnp.float32)
    rows = jnp.concatenate([a, b, c, a, b, a, unused], axis=0)
    change = jnp.dot(
        factor.astype(jnp.bfloat16), rows.astype(jnp.bfloat16), preferred_element_type=jnp.float32
    )
    left = jnp.concatenate([(left - change[:, :n])[BLOCK:], tile], axis=0)
    right = jnp.concatenate([(right - change[:, n:])[BLOCK:], side_tile], axis=0)
    return pltpu.roll(left, n - BLOCK, 1), right, pltpu.roll(near, n - BLOCK, 1), near_side


def solve_kernel(total_ref, out_ref):
    n = out_ref.shape[0]
    row = lax.broadcasted_iota(jnp.int32, (n, n), 0)
    column = lax.broadcasted_iota(jnp.int32, (n, n), 1)
    left = total_ref[:n] + jnp.where(row == column, n - 1.0, 0.0)
    right = total_ref[n:].T
    state = (left, right, left[:BLOCK], right[:BLOCK])
    for _ in range(n // BLOCK):
        state = eliminate(*state)
    solved = state[1]
    out_ref[...] = solved - jnp.mean(solved, axis=0, keepdims=True)


def centred_coefficients(total):
    n = total.shape[1]
    return pl.pallas_call(
        solve_kernel,
        out_shape=jax.ShapeDtypeStruct((n, n), jnp.float32),
        cost_estimate=pl.CostEstimate(flops=40000000, bytes_accessed=200000, transcendentals=0),
        compiler_params=pltpu.CompilerParams(vmem_limit_bytes=8 * 1024 * 1024),
    )(total)


def relayout_kernel(row_ref, out_ref):
    out_ref[...] = row_ref[...].reshape(out_ref.shape)


def lane_rows(row):
    return pl.pallas_call(
        relayout_kernel,
        out_shape=jax.ShapeDtypeStruct((row.shape[1] // LANES, LANES), row.dtype),
        cost_estimate=pl.CostEstimate(flops=0, bytes_accessed=4 * row.size, transcendentals=0),
        compiler_params=pltpu.CompilerParams(vmem_limit_bytes=4 * 1024 * 1024),
    )(row)


def exchange(value, axes):
    return lax.all_to_all(value, axes, split_axis=0, concat_axis=0, tiled=True)


def spread_to(value, axes):
    count = lax.axis_size(axes)
    return exchange(jnp.broadcast_to(value[None], (count,) + value.shape), axes)


def total_of(partial):
    near = lax.axis_size(NEAR)
    piece = jnp.sum(exchange(partial.reshape(near, -1, partial.shape[1]), NEAR), axis=0)
    piece = jnp.sum(spread_to(piece, "z"), axis=0)
    return spread_to(piece, NEAR).reshape(partial.shape)


def on_device(
    states,
    batch_index,
    obs_pick,
    norm_gain,
    w_in,
    b_in,
    member_params,
    observed,
    perturbation,
    inv_sigma,
):
    members = lax.axis_size(MEM)
    width = w_in.shape[1]
    features = w_in.shape[0]
    step_count, rows = batch_index.shape
    picked = obs_pick.shape[1]
    own = lane_rows(member_params).reshape(-1, features)
    weights = lax.all_gather(own, "r", axis=0, tiled=True)
    weights, states = lax.optimization_barrier((weights, states))
    step_scale = DT * width ** (-0.5)
    current = states.astype(jnp.float32)
    for _ in range(2):
        layer = hidden_layer(current, norm_gain, w_in, b_in)
        current = current + step_scale * jnp.dot(layer, weights, preferred_element_type=jnp.float32)
    feature_ids = lax.broadcasted_iota(jnp.int32, (step_count, features, picked), 1)
    selector = (feature_ids == obs_pick[:, None, :]).astype(jnp.float32)
    state_ids = lax.broadcasted_iota(jnp.int32, (step_count, rows, states.shape[0]), 2)
    row_selector = (state_ids == batch_index[:, :, None]).astype(jnp.float32)
    narrowed = jnp.einsum("bs,ksf->kbf", current, selector, precision=HIGHEST)
    predicted = jnp.einsum("kib,kbf->kif", row_selector, narrowed, precision=HIGHEST)
    scaled = predicted * inv_sigma
    weighted = scaled.astype(jnp.bfloat16)
    misfit_w = (
        observed.astype(jnp.float32) * inv_sigma + perturbation[0].astype(jnp.float32) - scaled
    ).astype(jnp.bfloat16)
    misfit_lanes = jnp.sum(jnp.square(misfit_w.astype(jnp.float32)), axis=(0, 1))
    misfit_local = jnp.dot(
        misfit_lanes[None], jnp.ones((picked, members), jnp.float32), precision=HIGHEST
    )
    entries = members * step_count * rows * lax.axis_size("r") * picked
    pairs = (members, -1, 2, picked)
    pairs = (members, -1, 2, picked)
    sent = [weighted.reshape(pairs), misfit_w.reshape(pairs), own.reshape(pairs)]
    depth = sent[0].shape[1]
    arrived = exchange(jnp.concatenate(sent, axis=1), MEM)
    gathered = arrived[:, :depth].astype(jnp.float32)
    misfit_here = arrived[:, depth : 2 * depth]
    param_block = arrived[:, 2 * depth :]
    param_block, gathered = lax.optimization_barrier((param_block, gathered))
    anomaly = (gathered - jnp.mean(gathered, axis=0)).astype(jnp.bfloat16)
    both = jnp.concatenate([anomaly, misfit_here], axis=0)
    partial = lax.dot_general(
        both, anomaly, (((1, 2, 3), (1, 2, 3)), ((), ())), preferred_element_type=jnp.float32
    )
    unit = lax.broadcasted_iota(jnp.int32, partial.shape, 0) == lax.broadcasted_iota(
        jnp.int32, partial.shape, 1
    )
    partial = partial + jnp.where(unit, (members - 1) / entries, 0.0) * misfit_local
    total = total_of(partial)
    centred = centred_coefficients(total)
    params_f = param_block.astype(jnp.float32)
    change = jnp.einsum("kj,kabp->jabp", centred, params_f, precision=HIGHEST)
    renewed = (params_f + change).astype(jnp.bfloat16)
    return exchange(renewed, MEM).reshape(member_params.shape)


def solution(mesh):
    fine = Mesh(mesh.devices.reshape(4, 16, 2, 4), ("x", "z", "c", "r"))
    placed = (
        P("r", None),
        P(None, "r"),
        P(),
        P(),
        P(),
        P(),
        P(OWNERS, "r"),
        P(None, "r", None),
        P(OWNERS, None, "r", None),
        P(None, "r", None),
    )
    return jax.shard_map(
        on_device, mesh=fine, in_specs=placed, out_specs=P(OWNERS, "r"), check_vma=False
    )
```

```python
import jax
import jax.numpy as jnp
from jax import lax
from jax.experimental import pallas as pl
from jax.experimental.pallas import tpu as pltpu
from jax.sharding import Mesh
from jax.sharding import PartitionSpec as P

EPS = 1e-06
DT = 0.5
MEM = ("z", "x", "c")
OWNERS = ("x", "z", "c")
NEAR = ("x", "c", "r")
BLOCK = 8
LANES = 128
HIGHEST = lax.Precision.HIGHEST


def hidden_layer(state, norm_gain, w_in, b_in):
    normed = (
        state * lax.rsqrt(jnp.mean(state * state, axis=-1, keepdims=True) + EPS) * norm_gain
    ).astype(jnp.bfloat16)
    return jax.nn.gelu(jnp.dot(normed, w_in, preferred_element_type=jnp.float32) + b_in).astype(
        jnp.bfloat16
    )


def wide(value):
    return jnp.broadcast_to(value, (BLOCK, value.shape[1] if value.shape[1] > 1 else LANES))


def split(value):
    head = value.astype(jnp.bfloat16).astype(jnp.float32)
    rest = value - head
    middle = rest.astype(jnp.bfloat16).astype(jnp.float32)
    return head, middle, rest - middle


def pivot_rows(left, right):
    cols = [wide(left[:, q : q + 1]) for q in range(BLOCK)]
    pivots = [[wide(cols[q][p : p + 1]) for q in range(p + 1)] for p in range(BLOCK)]
    top = [wide(left[p : p + 1]) for p in range(BLOCK)]
    side = [wide(right[p : p + 1]) for p in range(BLOCK)]
    factors = {}
    for p in range(0, BLOCK, 2):
        a, b, d = pivots[p][p], pivots[p + 1][p], pivots[p + 1][p + 1]
        inverse = 1.0 / (a * d - b * b)
        ia, ib, id_ = d * inverse, -(b * inverse), a * inverse
        for q in range(p + 2, BLOCK):
            factors[q, p] = f = pivots[q][p] * ia + pivots[q][p + 1] * ib
            factors[q, p + 1] = g = pivots[q][p] * ib + pivots[q][p + 1] * id_
            for c in range(p + 2, q + 1):
                pivots[q][c] = pivots[q][c] - f * pivots[c][p] - g * pivots[c][p + 1]
            top[q] = top[q] - f * top[p] - g * top[p + 1]
            side[q] = side[q] - f * side[p] - g * side[p + 1]
        for rows in (top, side):
            rows[p], rows[p + 1] = ia * rows[p] + ib * rows[p + 1], ib * rows[p] + id_ * rows[p + 1]
    for p in reversed(range(2, BLOCK)):
        for q in range(p // 2 * 2):
            top[q] = top[q] - factors[p, q] * top[p]
            side[q] = side[q] - factors[p, q] * side[p]
    row = lax.broadcasted_iota(jnp.int32, left.shape, 0)
    tile, side_tile = top[0], side[0]
    for p in range(1, BLOCK):
        tile = jnp.where(row == p, top[p], tile)
        side_tile = jnp.where(row == p, side[p], side_tile)
    return tile, side_tile, top, side


def eliminate(left, right, tile, side_tile):
    n = left.shape[0]
    tile, side_tile, top, side = pivot_rows(tile, side_tile)
    near, near_side = left[BLOCK : 2 * BLOCK], right[BLOCK : 2 * BLOCK]
    cols = [wide(near[:, q : q + 1]) for q in range(BLOCK)]
    for q in range(BLOCK):
        near = near - cols[q] * top[q]
        near_side = near_side - cols[q] * side[q]
    column = lax.broadcasted_iota(jnp.int32, left.shape, 1)
    a, b, c = split(jnp.where(column < BLOCK, left, 0.0))
    factor = a
    for place, part in enumerate((a, a, b, b, c)):
        factor = factor + pltpu.roll(part, (place + 1) * BLOCK, 1)
    a, b, c = split(jnp.concatenate([tile, side_tile], axis=1))
    unused = jnp.zeros((n - 6 * BLOCK, 2 * n), jnp.float32)
    rows = jnp.concatenate([a, b, c, a, b, a, unused], axis=0)
    change = jnp.dot(
        factor.astype(jnp.bfloat16), rows.astype(jnp.bfloat16), preferred_element_type=jnp.float32
    )
    left = jnp.concatenate([(left - change[:, :n])[BLOCK:], tile], axis=0)
    right = jnp.concatenate([(right - change[:, n:])[BLOCK:], side_tile], axis=0)
    return pltpu.roll(left, n - BLOCK, 1), right, pltpu.roll(near, n - BLOCK, 1), near_side


def solve_kernel(total_ref, out_ref):
    n = out_ref.shape[0]
    row = lax.broadcasted_iota(jnp.int32, (n, n), 0)
    column = lax.broadcasted_iota(jnp.int32, (n, n), 1)
    left = total_ref[:n] + jnp.where(row == column, n - 1.0, 0.0)
    right = total_ref[n:].T
    state = (left, right, left[:BLOCK], right[:BLOCK])
    for _ in range(n // BLOCK):
        state = eliminate(*state)
    solved = state[1]
    out_ref[...] = solved - jnp.mean(solved, axis=0, keepdims=True)


def centred_coefficients(total):
    n = total.shape[1]
    return pl.pallas_call(
        solve_kernel,
        out_shape=jax.ShapeDtypeStruct((n, n), jnp.float32),
        cost_estimate=pl.CostEstimate(flops=40000000, bytes_accessed=200000, transcendentals=0),
        compiler_params=pltpu.CompilerParams(vmem_limit_bytes=8 * 1024 * 1024),
    )(total)


def relayout_kernel(row_ref, out_ref):
    out_ref[...] = row_ref[...].reshape(out_ref.shape)


def lane_rows(row):
    return pl.pallas_call(
        relayout_kernel,
        out_shape=jax.ShapeDtypeStruct((row.shape[1] // LANES, LANES), row.dtype),
        cost_estimate=pl.CostEstimate(flops=0, bytes_accessed=4 * row.size, transcendentals=0),
        compiler_params=pltpu.CompilerParams(vmem_limit_bytes=4 * 1024 * 1024),
    )(row)


def exchange(value, axes):
    return lax.all_to_all(value, axes, split_axis=0, concat_axis=0, tiled=True)


def spread_to(value, axes):
    count = lax.axis_size(axes)
    return exchange(jnp.broadcast_to(value[None], (count,) + value.shape), axes)


def total_of(partial):
    near = lax.axis_size(NEAR)
    piece = jnp.sum(exchange(partial.reshape(near, -1, partial.shape[1]), NEAR), axis=0)
    piece = jnp.sum(spread_to(piece, "z"), axis=0)
    return spread_to(piece, NEAR).reshape(partial.shape)


def on_device(
    states,
    batch_index,
    obs_pick,
    norm_gain,
    w_in,
    b_in,
    member_params,
    observed,
    perturbation,
    inv_sigma,
):
    members = lax.axis_size(MEM)
    width = w_in.shape[1]
    features = w_in.shape[0]
    step_count, rows = batch_index.shape
    picked = obs_pick.shape[1]
    own = lane_rows(member_params).reshape(-1, features)
    weights = lax.all_gather(own, "r", axis=0, tiled=True)
    weights, states = lax.optimization_barrier((weights, states))
    step_scale = DT * width ** (-0.5)
    current = states.astype(jnp.float32)
    for _ in range(2):
        layer = hidden_layer(current, norm_gain, w_in, b_in)
        current = current + step_scale * jnp.dot(layer, weights, preferred_element_type=jnp.float32)
    feature_ids = lax.broadcasted_iota(jnp.int32, (step_count, features, picked), 1)
    selector = (feature_ids == obs_pick[:, None, :]).astype(jnp.float32)
    state_ids = lax.broadcasted_iota(jnp.int32, (step_count, rows, states.shape[0]), 2)
    row_selector = (state_ids == batch_index[:, :, None]).astype(jnp.float32)
    narrowed = jnp.einsum("bs,ksf->kbf", current, selector, precision=HIGHEST)
    predicted = jnp.einsum("kib,kbf->kif", row_selector, narrowed, precision=HIGHEST)
    scaled = predicted * inv_sigma
    weighted = scaled.astype(jnp.bfloat16)
    misfit_w = (
        observed.astype(jnp.float32) * inv_sigma + perturbation[0].astype(jnp.float32) - scaled
    ).astype(jnp.bfloat16)
    misfit_lanes = jnp.sum(jnp.square(misfit_w.astype(jnp.float32)), axis=(0, 1))
    misfit_local = jnp.dot(
        misfit_lanes[None], jnp.ones((picked, members), jnp.float32), precision=HIGHEST
    )
    entries = members * step_count * rows * lax.axis_size("r") * picked
    pairs = (members, -1, 2, picked)
    pairs = (members, -1, 2, picked)
    sent = [weighted.reshape(pairs), misfit_w.reshape(pairs), own.reshape(pairs)]
    depth = sent[0].shape[1]
    sent, misfit_local = lax.optimization_barrier((jnp.concatenate(sent, axis=1), misfit_local))
    arrived = exchange(sent, MEM)
    gathered = arrived[:, :depth].astype(jnp.float32)
    misfit_here = arrived[:, depth : 2 * depth]
    param_block = arrived[:, 2 * depth :]
    param_block, gathered = lax.optimization_barrier((param_block, gathered))
    anomaly = (gathered - jnp.mean(gathered, axis=0)).astype(jnp.bfloat16)
    both = jnp.concatenate([anomaly, misfit_here], axis=0)
    partial = lax.dot_general(
        both, anomaly, (((1, 2, 3), (1, 2, 3)), ((), ())), preferred_element_type=jnp.float32
    )
    unit = lax.broadcasted_iota(jnp.int32, partial.shape, 0) == lax.broadcasted_iota(
        jnp.int32, partial.shape, 1
    )
    partial = partial + jnp.where(unit, (members - 1) / entries, 0.0) * misfit_local
    total = total_of(partial)
    centred = centred_coefficients(total)
    params_f = param_block.astype(jnp.float32)
    change = jnp.einsum("kj,kabp->jabp", centred, params_f, precision=HIGHEST)
    renewed = (params_f + change).astype(jnp.bfloat16)
    return exchange(renewed, MEM).reshape(member_params.shape)


def solution(mesh):
    fine = Mesh(mesh.devices.reshape(4, 16, 2, 4), ("x", "z", "c", "r"))
    placed = (
        P("r", None),
        P(None, "r"),
        P(),
        P(),
        P(),
        P(),
        P(OWNERS, "r"),
        P(None, "r", None),
        P(OWNERS, None, "r", None),
        P(None, "r", None),
    )
    return jax.shard_map(
        on_device, mesh=fine, in_specs=placed, out_specs=P(OWNERS, "r"), check_vma=False
    )
```
